32 devices in a mesh: region: 16 (over z, x, core), level: 2 (over y).
Axes of the slice: x: 2, y: 2, z: 4, core: 2. Of those that a mesh axis runs over, the one named last changes fastest.
Arguments:
- prior_samples: bfloat16 [256, 16, 24576], P('region', 'level'), may hold values from -6 to 6
- measured_site: int32 [8192], P('region'), may hold values from 0 to 24575
- measured_datum: float32 [8192], P('region'), may hold values from -6 to 6
- inverse_variance: float32 [8192], P('region'), may hold values from 0.5 to 8
- active_slots: int32 [16], P('region'), may hold values from 256 to 512
- cutoff_distance: int32 [16], P('region'), may hold values from 128 to 256
Outputs:
- analysis: bfloat16 [256, 16, 24576], P('region', 'level')
The draws below stay inside these ranges and needn't reach their ends.
Inputs may be any that keep to these rules, and one draw needn't show every extreme that they name: measured_site[o] = level * 1536 + cell within its region, for a level below 16. Slots of region r at or past active_slots[r] are empty and are ignored.
All inputs are finite; a program needn't handle non-finite values.
Results may differ from the reference program's by a relative error of at most 0.00115.
The reference program's roundings to bfloat16 on the way count: a program that leaves them out, or rounds other values in their place, can miss the bound.
Values may be sent and summed in bfloat16 or wider, within the bound.
No kernel may reach another device: no remote copies, remote signals or barrier semaphores. Data moves between devices by JAX's collectives and lax.ppermute only.
A program may use at most 256 MiB of HBM per device.

```python
import math
import jax
import jax.numpy as jnp
from jax import lax

SAMPLE_SIZE = 256
COARSE = 6
SPACING = 256
OBS_DEV = 512
NS_ITERS = 5
PTS_DEV = 1536
REGIONS = 16
HEIGHT_TIERS = 16
GRID_SITES = 24576
NOBS = 8192


def plant(values, own_key, smallest, high):
    longest = values.shape.index(max(values.shape))
    spots = []
    for shift in (0, 1):
        where = [jax.random.randint(jax.random.fold_in(own_key, axis), (), 0, length) for axis, length in enumerate(values.shape)]
        where[longest] = (where[longest] + shift) % values.shape[longest]
        spots.append(tuple(where))
    return values.at[spots[0]].set(smallest).at[spots[1]].set(high)


def levels(rng, extent, split, least, top_value):
    level, own = 1.0, jax.random.fold_in(rng, 6)
    for dim, parts in split:
        steps = jnp.exp(jax.random.uniform(jax.random.fold_in(own, dim), (parts,), jnp.float32, least / len(split), top_value / len(split)))
        level = level * jnp.repeat(steps, extent[dim] // parts).reshape([-1 if axis == dim else 1 for axis in range(len(extent))])
    return level


def noise(own_key, shape, scale, bound, cuts=(), kind=jnp.bfloat16):
    drawn = scale * jax.random.normal(own_key, shape, jnp.float32)
    if cuts:
        drawn = drawn * levels(own_key, shape, cuts, -0.22, 0.18)
    return jnp.clip(drawn, -bound, bound).astype(kind)


def setup_inputs(seed: int = 0) -> dict:
    streams_of = jax.random.split(jax.random.key(seed), 7)
    prior_samples = noise(streams_of[0], (SAMPLE_SIZE, HEIGHT_TIERS, GRID_SITES), 1.0, 6.0, ((0, 16), (1, 2)))
    measured_site = plant(jax.random.randint(streams_of[1], (NOBS,), 0, HEIGHT_TIERS * PTS_DEV), jax.random.fold_in(streams_of[1], 1), 0, (HEIGHT_TIERS * PTS_DEV) - 1).astype(jnp.int32)
    measured_datum = noise(streams_of[2], (NOBS,), 1.0, 6.0, ((0, 16),), jnp.float32)
    inverse_variance = jnp.clip(jnp.exp(math.log(8.0) - 2.7725887 * jax.random.uniform(streams_of[3], (NOBS,), jnp.float32) ** levels(streams_of[3], (NOBS,), ((0, 16),), -0.2, 0.2)), 0.5, 8.0)
    active_slots = plant(jax.random.randint(streams_of[4], (REGIONS,), OBS_DEV // 2, OBS_DEV + 1), jax.random.fold_in(streams_of[4], 1), OBS_DEV // 2, OBS_DEV).astype(jnp.int32)
    cutoff_distance = plant(jax.random.randint(streams_of[5], (REGIONS,), SPACING // 2, SPACING + 1), jax.random.fold_in(streams_of[5], 1), SPACING // 2, SPACING).astype(jnp.int32)
    return dict(prior_samples=prior_samples, measured_site=measured_site, measured_datum=measured_datum, inverse_variance=inverse_variance, active_slots=active_slots, cutoff_distance=cutoff_distance)


inflation = 1.1

def local_products(window, records, radius_cells):
    values = window.astype(jnp.float32)
    centre = lax.optimization_barrier(jnp.mean(values, axis=0))
    departure = values - centre[None, :]
    innovation = records[3] * (records[0] - centre)
    coarse = (SPACING // 2 + SPACING * jnp.arange(COARSE, dtype=jnp.int32)).astype(jnp.float32)
    distance = (records[2][None, :] - coarse[:, None]) / radius_cells
    root_weight = jnp.sqrt(jnp.exp(-0.5 * distance * distance) * records[1][None, :])
    scaled = (departure[None, :, :] * root_weight[:, None, :]).astype(jnp.bfloat16)
    weighted = (root_weight * innovation[None, :]).astype(jnp.bfloat16)
    scaled_wide = scaled.astype(jnp.float32)
    gram_matrix = jnp.einsum('cjo,cmo->cjm', scaled_wide, scaled_wide, precision=lax.Precision.HIGHEST)
    right_side = jnp.einsum('cjo,co->cj', scaled_wide, weighted.astype(jnp.float32), precision=lax.Precision.HIGHEST)
    return (gram_matrix, right_side)

def ensemble_weights(gram_matrix, right_side):
    sample_runs = gram_matrix.shape[-1]
    identity = jnp.eye(sample_runs, dtype=jnp.float32)
    shifted = gram_matrix + (sample_runs - 1) / inflation * identity[None]
    frobenius = jnp.sqrt(lax.optimization_barrier(jnp.sum(shifted * shifted, axis=(1, 2))))
    iterate = shifted / frobenius[:, None, None]
    inverse = jnp.broadcast_to(identity, shifted.shape)
    for turn_index in range(NS_ITERS):
        factor = 1.5 * identity[None] - 0.5 * jnp.matmul(inverse, iterate, precision=lax.Precision.HIGHEST)
        iterate = jnp.matmul(iterate, factor, precision=lax.Precision.HIGHEST)
        inverse = jnp.matmul(factor, inverse, precision=lax.Precision.HIGHEST)
    spread = inverse * jnp.sqrt((sample_runs - 1.0) / frobenius)[:, None, None]
    inner_step = jnp.einsum('cjm,cm->cj', inverse, right_side, precision=lax.Precision.HIGHEST)
    centre = jnp.einsum('cjm,cm->cj', inverse, inner_step, precision=lax.Precision.HIGHEST) / frobenius[:, None]
    weights = spread + centre[:, :, None]
    return (weights - lax.optimization_barrier(jnp.mean(weights, axis=1, keepdims=True)) + 1.0 / sample_runs).astype(jnp.bfloat16)

def transform(vertical_profiles, extended):
    sample_runs, height_tiers, grid_sites = vertical_profiles.shape
    half_block = grid_sites // (2 * COARSE)
    shaped = vertical_profiles.astype(jnp.float32).reshape(sample_runs, height_tiers, COARSE, 2, half_block)
    ext_wide = extended.astype(jnp.float32)
    middle = jnp.einsum('jlmqp,mjk->klmqp', shaped, ext_wide[1:COARSE + 1], precision=lax.Precision.HIGHEST)
    before = jnp.einsum('jlmp,mjk->klmp', shaped[:, :, :, 0], ext_wide[:COARSE], precision=lax.Precision.HIGHEST)
    beyond = jnp.einsum('jlmp,mjk->klmp', shaped[:, :, :, 1], ext_wide[2:], precision=lax.Precision.HIGHEST)
    offset = jnp.arange(half_block, dtype=jnp.float32)
    frac_low = (offset + half_block) / (2 * half_block)
    frac_high = offset / (2 * half_block)
    low_half = (1.0 - frac_low) * before + frac_low * middle[:, :, :, 0]
    high_half = (1.0 - frac_high) * middle[:, :, :, 1] + frac_high * beyond
    return jnp.stack([low_half, high_half], axis=3).reshape(sample_runs, height_tiers, grid_sites).astype(jnp.bfloat16)

def reference(prior_samples, measured_site, measured_datum, inverse_variance, active_slots, cutoff_distance):
    sample_runs, height_tiers, grand_accumulated = prior_samples.shape
    grid_sites = COARSE * SPACING
    regions = grand_accumulated // grid_sites
    slots = measured_site.shape[0] // regions
    slot_index = jnp.arange(regions * slots, dtype=jnp.int32)
    region_of = (slot_index // slots).astype(jnp.int32)
    live = slot_index % slots < active_slots[region_of]
    level_of = measured_site // grid_sites
    point_of = measured_site % grid_sites
    linear_offset = (level_of * grand_accumulated + region_of * grid_sites + point_of).astype(jnp.int32)
    sample_fields = jnp.take(prior_samples.reshape(sample_runs, height_tiers * grand_accumulated), linear_offset, axis=1)
    sample_fields = jnp.where(live[None, :], sample_fields, jnp.zeros_like(sample_fields))
    live_f = live.astype(jnp.float32)
    records = jnp.stack([measured_datum, inverse_variance * live_f, point_of.astype(jnp.float32), live_f])
    ensemble_by = sample_fields.reshape(sample_runs, regions, slots)
    records_by = records.reshape(4, regions, slots)
    shifts = jnp.array([-grid_sites, 0, grid_sites], dtype=jnp.float32)

    def one_region(patch_ordinal):
        neighbours = jnp.stack([(patch_ordinal - 1) % regions, patch_ordinal, (patch_ordinal + 1) % regions]).astype(jnp.int32)
        window = jnp.take(ensemble_by, neighbours, axis=1).reshape(sample_runs, 3 * slots)
        near = jnp.take(records_by, neighbours, axis=1)
        position = near[2] + shifts[:, None]
        near = jnp.stack([near[0], near[1], position, near[3]]).reshape(4, 3 * slots)
        gram_matrix, right_side = local_products(window, near, cutoff_distance[patch_ordinal].astype(jnp.float32))
        return ensemble_weights(gram_matrix, right_side)
    weights = lax.map(one_region, jnp.arange(regions, dtype=jnp.int32))
    extended = jnp.concatenate([jnp.roll(weights[:, -1:], 1, axis=0), weights, jnp.roll(weights[:, :1], -1, axis=0)], axis=1)

    def one_block(region_item):
        patch_ordinal, ext_block = region_item
        vertical_profiles = lax.dynamic_slice_in_dim(prior_samples, (patch_ordinal * grid_sites).astype(jnp.int32), grid_sites, axis=2)
        return transform(vertical_profiles, ext_block)
    blocks = lax.map(one_block, (jnp.arange(regions, dtype=jnp.int32), extended))
    return jnp.transpose(blocks, (1, 2, 0, 3)).reshape(sample_runs, height_tiers, grand_accumulated)
```

```python
import functools

import jax
import jax.numpy as jnp
from jax import lax
from jax.experimental import pallas as pl
from jax.experimental.pallas import tpu as pltpu
from jax.sharding import PartitionSpec as P

COARSE = 6
SPACING = 256
NS_ITERS = 5
HALVES = 2
LANES = 128

inflation = 1.1


def gather_kernel(cell_ref, level_ref, fields_ref, out_ref):
    members, tiers, cells = fields_ref.shape
    slots = cell_ref.shape[-1]
    rows = lax.broadcasted_iota(jnp.int32, (cells, slots), 0)
    chosen = jnp.where(rows == cell_ref[0], 1.0, 0.0).astype(jnp.bfloat16)
    fields = fields_ref[...].reshape(members * tiers, cells)
    found = jnp.dot(fields, chosen, preferred_element_type=jnp.float32)
    found = found.reshape(members, tiers, slots)
    tier = lax.broadcasted_iota(jnp.int32, (members, tiers, slots), 1)
    found = jnp.where(tier == level_ref[...], found, 0.0)
    out_ref[0] = jnp.sum(found, axis=1).astype(jnp.bfloat16)


def gather_observed(prior, cell, level):
    members, tiers, total = prior.shape
    regions, _, slots = cell.shape
    cells = total // regions
    return pl.pallas_call(
        gather_kernel,
        grid=(regions,),
        in_specs=[
            pl.BlockSpec((1, 1, slots), lambda r: (r, 0, 0)),
            pl.BlockSpec((1, 1, slots), lambda r: (r, 0, 0)),
            pl.BlockSpec((members, tiers, cells), lambda r: (0, 0, r)),
        ],
        out_specs=pl.BlockSpec((1, members, slots), lambda r: (r, 0, 0)),
        out_shape=jax.ShapeDtypeStruct((regions, members, slots), jnp.bfloat16),
        name="gather_observed",
    )(cell, level, prior)


def transform_kernel(first, chips, where_ref, *refs):
    pieces = refs[:chips]
    other_ref, matrices_ref, keep_ref, give_ref, work = refs[chips:]
    _, members, tiers, cells = other_ref.shape
    total = chips * 2 * members
    rows = members * tiers
    core = where_ref[chips]
    for p in range(chips):
        chip = where_ref[p]
        own = pieces[p][:, :, pl.ds(pl.multiple_of(core * cells, LANES), cells)]
        start = pl.multiple_of((chip * 2 + core) * rows, 8)
        own = own.astype(jnp.float32).reshape(rows, cells)
        other = other_ref[p].astype(jnp.float32).reshape(rows, cells)
        beside = pl.multiple_of((chip * 2 + 1 - core) * rows, 8)
        for b in range(cells // LANES):
            span = slice(b * LANES, (b + 1) * LANES)
            work[b, pl.ds(start, rows), :] = own[:, span]
            work[b, pl.ds(beside, rows), :] = other[:, span]
    offset = lax.broadcasted_iota(jnp.int32, (1, LANES), 1).astype(jnp.float32)
    half = SPACING // 2
    for b in range(cells // LANES):
        block = first * (cells // LANES) + b
        low = (block + 1) // 2
        skip = (block * LANES + half) % SPACING
        frac = (offset + skip) / SPACING
        frac = jnp.concatenate([frac] * tiers, axis=1)
        values = jnp.concatenate(
            [
                work[b, pl.ds(t, total, stride=tiers), :].astype(jnp.bfloat16)
                for t in range(tiers)
            ],
            axis=1,
        )
        base = low - (first * (cells // LANES) + 1) // 2
        under = jnp.dot(matrices_ref[base], values, preferred_element_type=jnp.float32)
        over = jnp.dot(matrices_ref[base + 1], values, preferred_element_type=jnp.float32)
        mixed = (1.0 - frac) * under + frac * over
        for t in range(tiers):
            work[b, pl.ds(t, total, stride=tiers), :] = mixed[:, t * LANES : (t + 1) * LANES]
    for d in range(chips):
        for side, out_ref in ((core, keep_ref), (1 - core, give_ref)):
            start = pl.multiple_of((d * 2 + side) * rows, 8)
            for b in range(cells // LANES):
                block = work[b, pl.ds(start, rows), :].reshape(members, tiers, LANES)
                out_ref[d, :, :, b * LANES : (b + 1) * LANES] = block.astype(jnp.bfloat16)


def transform(first, where, pieces, other, matrices):
    chips, members, tiers, cells = other.shape
    out = jax.ShapeDtypeStruct(other.shape, jnp.bfloat16)
    whole = pl.BlockSpec(memory_space=pltpu.VMEM)
    return pl.pallas_call(
        functools.partial(transform_kernel, first, chips),
        in_specs=[pl.BlockSpec(memory_space=pltpu.SMEM)] + [whole] * (chips + 2),
        out_specs=[whole, whole],
        out_shape=[out, out],
        scratch_shapes=[pltpu.VMEM((cells // LANES, chips * 2 * members * tiers, LANES), jnp.float32)],
        name=f"transform_{first}",
    )(where, *pieces, other, matrices)


def local_products(window, records, radius_cells, coarse):
    values = window.astype(jnp.float32)
    centre = jnp.mean(values, axis=0)
    departure = values - centre[None, :]
    innovation = records[3] * (records[0] - centre)
    distance = (records[2][None, :] - coarse[:, None]) / radius_cells
    root_weight = jnp.sqrt(jnp.exp(-0.5 * distance * distance) * records[1][None, :])
    scaled = (departure[None, :, :] * root_weight[:, None, :]).astype(jnp.bfloat16)
    weighted = (root_weight * innovation[None, :]).astype(jnp.bfloat16)
    gram_matrix = jnp.einsum("cjo,cmo->cjm", scaled, scaled, preferred_element_type=jnp.float32)
    right_side = jnp.einsum("cjo,co->cj", scaled, weighted, preferred_element_type=jnp.float32)
    return (gram_matrix, right_side)


def ensemble_weights(gram_matrix, right_side):
    sample_runs = gram_matrix.shape[-1]
    identity = jnp.eye(sample_runs, dtype=jnp.float32)
    shifted = gram_matrix + (sample_runs - 1) / inflation * identity[None]
    frobenius = jnp.sqrt(jnp.sum(shifted * shifted, axis=(1, 2)))
    iterate = shifted / frobenius[:, None, None]
    inverse = 1.5 * identity[None] - 0.5 * iterate
    high = lax.Precision.HIGHEST
    iterate = jnp.matmul(iterate, inverse, precision=high)
    for turn in range(1, NS_ITERS):
        factor = 1.5 * identity[None] - 0.5 * jnp.matmul(inverse, iterate, precision=high)
        if turn < NS_ITERS - 1:
            iterate = jnp.matmul(iterate, factor, precision=high)
        inverse = jnp.matmul(factor, inverse, precision=high)
    spread = inverse * jnp.sqrt((sample_runs - 1.0) / frobenius)[:, None, None]
    inner_step = jnp.einsum("cjm,cm->cj", inverse, right_side, precision=high)
    centre = jnp.einsum("cjm,cm->cj", inverse, inner_step, precision=high) / frobenius[:, None]
    weights = spread + centre[:, :, None]
    weights = weights - jnp.mean(weights, axis=1, keepdims=True) + 1.0 / sample_runs
    return jnp.swapaxes(weights, 1, 2).astype(jnp.bfloat16)


def local(
    prior_samples, measured_site, measured_datum, inverse_variance, active_slots, cutoff_distance
):
    members, tiers, total = prior_samples.shape
    regions = lax.axis_size("region")
    levels = lax.axis_size("level")
    grid_sites = COARSE * SPACING
    slots = measured_site.shape[0]
    me = lax.axis_index("region")
    tier_rank = lax.axis_index("level")
    chips = regions // 2
    across = chips // 4
    core = me % 2
    chip = me // 2
    cells = grid_sites // HALVES
    steps = [(dz, dx) for dz in (3, 2, 1, 0) for dx in reversed(range(across))]

    def target(chip_index, dz, dx):
        return ((chip_index // across) ^ dz) * across + ((chip_index % across) ^ dx)

    def swap(block, dz, dx):
        if (dz, dx) == (0, 0):
            return block
        pairs = [(i, target(i // 2, dz, dx) * 2 + i % 2) for i in range(regions)]
        return lax.ppermute(block, "region", pairs)

    def swap_core(block):
        return lax.ppermute(block, "region", [(i, i ^ 1) for i in range(regions)])

    partners = [target(chip, dz, dx) for dz, dx in steps]
    where = jnp.stack(partners + [core]).astype(jnp.int32)

    def piece(source, chip_index, half):
        start = chip_index * (2 * grid_sites) + half * cells
        return jnp.concatenate(
            [
                lax.dynamic_slice_in_dim(source, start + c * grid_sites, cells, axis=2)
                for c in range(2)
            ],
            axis=2,
        )

    live = jnp.arange(slots, dtype=jnp.int32) < active_slots[0]
    live_f = live.astype(jnp.float32)
    records = jnp.stack(
        [
            jnp.where(live, measured_site, -1).astype(jnp.float32),
            measured_datum,
            inverse_variance * live_f,
        ]
    )
    table = lax.all_to_all(
        jnp.broadcast_to(records[None], (regions,) + records.shape),
        "region",
        split_axis=0,
        concat_axis=0,
        tiled=True,
    )
    sites = table[:, 0:1].astype(jnp.int32)
    cell = jnp.where(sites < 0, -1, sites % grid_sites)
    tier = jnp.where(sites < 0, -1, sites // grid_sites - tier_rank * tiers)
    observed = gather_observed(prior_samples, cell, tier)
    flip = [(i, (i + 1) % levels) for i in range(levels)]
    observed = observed + lax.ppermute(observed, "level", flip)
    observed = lax.all_to_all(observed, "region", split_axis=0, concat_axis=0, tiled=True)
    observed = observed.reshape(regions * members, slots)
    up = [(i, (i + 1) % regions) for i in range(regions)]
    down = [(target_, source) for source, target_ in up]
    window = jnp.concatenate(
        [
            lax.ppermute(observed, "region", up),
            observed,
            lax.ppermute(observed, "region", down),
        ],
        axis=1,
    )
    near = []
    for shift in (-1, 0, 1):
        row = lax.dynamic_index_in_dim(table, (me + shift) % regions, axis=0, keepdims=False)
        site = row[0].astype(jnp.int32)
        here = (site >= 0).astype(jnp.float32)
        point = jnp.where(site < 0, 0, site % grid_sites).astype(jnp.float32)
        near.append(jnp.stack([row[1], row[2], point + shift * grid_sites, here]))
    near = jnp.concatenate(near, axis=1)
    share = COARSE // levels
    coarse = (
        SPACING // 2 + SPACING * (tier_rank * share + jnp.arange(share, dtype=jnp.int32))
    ).astype(jnp.float32)
    gram_matrix, right_side = local_products(
        window, near, cutoff_distance[0].astype(jnp.float32), coarse
    )
    weights = ensemble_weights(gram_matrix, right_side)
    opposite = lax.ppermute(weights, "level", flip)
    weights = jnp.where(
        tier_rank == 0,
        jnp.concatenate([weights, opposite]),
        jnp.concatenate([opposite, weights]),
    )
    before = lax.ppermute(weights[-1:], "region", up)
    beyond = lax.ppermute(weights[:1], "region", down)

    arrived = []
    for half in range(HALVES):
        arrived.append([swap(piece(prior_samples, d, half), *s) for d, s in zip(partners, steps)])
    analysis = jnp.zeros(prior_samples.shape, jnp.bfloat16)
    for half in range(HALVES):
        pieces = arrived[half]
        other = swap_core(
            jnp.stack(
                [
                    lax.dynamic_slice_in_dim(b, (1 - core) * cells, cells, axis=2)
                    for b in pieces
                ]
            )
        )
        if half == 0:
            matrices = jnp.concatenate([before, weights[: COARSE // 2 + 1]])
        else:
            matrices = jnp.concatenate([weights[COARSE // 2 - 1 :], beyond])
        keep, give = transform(half, where, pieces, other, matrices)
        got = swap_core(give)
        left = jnp.where(core == 0, keep, got)
        right = jnp.where(core == 0, got, keep)
        for d, s in zip(partners, steps):
            block = jnp.concatenate(
                [
                    lax.dynamic_index_in_dim(side, d, axis=0, keepdims=False)
                    for side in (left, right)
                ],
                axis=2,
            )
            block = swap(block, *s)
            start = d * (2 * grid_sites) + half * cells
            for c in range(2):
                analysis = lax.dynamic_update_slice_in_dim(
                    analysis,
                    block[:, :, c * cells : (c + 1) * cells],
                    start + c * grid_sites,
                    axis=2,
                )
    return analysis


def solution(mesh):
    return jax.shard_map(
        local,
        mesh=mesh,
        in_specs=(
            P("region", "level", None),
            P("region"),
            P("region"),
            P("region"),
            P("region"),
            P("region"),
        ),
        out_specs=P("region", "level", None),
        check_vma=False,
    )
```

```python
import functools

import jax
import jax.numpy as jnp
from jax import lax
from jax.experimental import pallas as pl
from jax.experimental.pallas import tpu as pltpu
from jax.sharding import PartitionSpec as P


COARSE = 6
SPACING = 256
NS_ITERS = 5
HALVES = 2
LANES = 128

inflation = 1.1


def gather_kernel(cell_ref, level_ref, fields_ref, out_ref):
    members, tiers, cells = fields_ref.shape
    slots = cell_ref.shape[-1]
    rows = lax.broadcasted_iota(jnp.int32, (cells, slots), 0)
    chosen = jnp.where(rows == cell_ref[0], 1.0, 0.0).astype(jnp.bfloat16)
    fields = fields_ref[...].reshape(members * tiers, cells)
    found = jnp.dot(fields, chosen, preferred_element_type=jnp.float32)
    found = found.reshape(members, tiers, slots)
    tier = lax.broadcasted_iota(jnp.int32, (members, tiers, slots), 1)
    found = jnp.where(tier == level_ref[...], found, 0.0)
    out_ref[0] = jnp.sum(found, axis=1).astype(jnp.bfloat16)


def gather_observed(prior, cell, level):
    members, tiers, total = prior.shape
    regions, _, slots = cell.shape
    cells = total // regions
    return pl.pallas_call(
        gather_kernel,
        grid=(regions,),
        in_specs=[
            pl.BlockSpec((1, 1, slots), lambda r: (r, 0, 0)),
            pl.BlockSpec((1, 1, slots), lambda r: (r, 0, 0)),
            pl.BlockSpec((members, tiers, cells), lambda r: (0, 0, r)),
        ],
        out_specs=pl.BlockSpec((1, members, slots), lambda r: (r, 0, 0)),
        out_shape=jax.ShapeDtypeStruct((regions, members, slots), jnp.bfloat16),
        name="gather_observed",
    )(cell, level, prior)


def copy_all(pairs, semaphore):
    copies = [pltpu.make_async_copy(a, b, semaphore.at[i]) for i, (a, b) in enumerate(pairs)]
    for copy in copies:
        copy.start()
    for copy in copies:
        copy.wait()


def moved(kernel, where, operands, out_shape, count, aliases=None):
    anywhere = pl.BlockSpec(memory_space=pl.ANY)
    several = isinstance(out_shape, list)
    return pl.pallas_call(
        kernel,
        in_specs=[pl.BlockSpec(memory_space=pltpu.SMEM)] + [anywhere] * len(operands),
        out_specs=[anywhere] * len(out_shape) if several else anywhere,
        out_shape=out_shape,
        scratch_shapes=[pltpu.SemaphoreType.DMA((count,))],
        input_output_aliases=aliases or {},
    )(where, *operands)


def cell_span(where_ref, rank, side, half, cells):
    chips = where_ref.shape[0] - 1
    core = where_ref[chips]
    region = where_ref[rank] * 2 + (core if side == 0 else 1 - core)
    return pl.ds(pl.multiple_of(region * (HALVES * cells) + half * cells, LANES), cells)


def cut(half, where, prior):
    chips = where.shape[0] - 1
    members, tiers, total = prior.shape
    cells = total // (2 * chips * HALVES)
    shape = jax.ShapeDtypeStruct((2, members, tiers, cells), prior.dtype)

    def kernel(where_ref, prior_ref, *refs):
        copy_all(
            [
                (
                    prior_ref.at[:, :, cell_span(where_ref, rank, side, half, cells)],
                    refs[rank].at[side],
                )
                for rank in range(chips)
                for side in range(2)
            ],
            refs[chips],
        )

    return moved(kernel, where, [prior], [shape] * chips, 2 * chips)


def hand(where, pieces):
    chips = len(pieces)
    shape = jax.ShapeDtypeStruct((chips,) + pieces[0].shape[1:], pieces[0].dtype)

    def kernel(where_ref, *refs):
        out_ref = refs[chips]
        copy_all([(refs[p].at[1], out_ref.at[p]) for p in range(chips)], refs[chips + 1])

    return moved(kernel, where, pieces, shape, chips)


def pack(where, keep, got):
    chips = keep.shape[0]
    shape = jax.ShapeDtypeStruct((2,) + keep.shape[1:], keep.dtype)

    def kernel(where_ref, keep_ref, got_ref, *refs):
        copy_all(
            [
                (source.at[p], refs[p].at[side])
                for p in range(chips)
                for side, source in enumerate((keep_ref, got_ref))
            ],
            refs[chips],
        )

    return moved(kernel, where, [keep, got], [shape] * chips, 2 * chips)


def join(half, where, blocks, shape, base):
    chips = len(blocks)
    cells = blocks[0].shape[-1]
    operands = blocks + ([] if base is None else [base])

    def kernel(where_ref, *refs):
        out_ref = refs[len(operands)]
        copy_all(
            [
                (
                    refs[rank].at[side],
                    out_ref.at[:, :, cell_span(where_ref, rank, side, half, cells)],
                )
                for rank in range(chips)
                for side in range(2)
            ],
            refs[len(operands) + 1],
        )

    aliases = None if base is None else {len(operands): 0}
    out = jax.ShapeDtypeStruct(shape, blocks[0].dtype)
    return moved(kernel, where, operands, out, 2 * chips, aliases)


def transform_kernel(first, chips, where_ref, *refs):
    pieces = refs[:chips]
    other_ref, matrices_ref, keep_ref, give_ref, work = refs[chips:]
    _, members, tiers, cells = other_ref.shape
    total = chips * 2 * members
    rows = members * tiers
    core = where_ref[chips]
    for p in range(chips):
        for side, piece in ((core, pieces[p][0]), (1 - core, other_ref[p])):
            start = pl.multiple_of((where_ref[p] * 2 + side) * rows, 8)
            piece = piece.astype(jnp.float32).reshape(rows, cells)
            for b in range(cells // LANES):
                work[b, pl.ds(start, rows), :] = piece[:, b * LANES : (b + 1) * LANES]
    offset = lax.broadcasted_iota(jnp.int32, (1, LANES), 1).astype(jnp.float32)
    half = SPACING // 2
    blocks = cells // LANES
    for b in range(blocks):
        block = first * blocks + b
        skip = (block * LANES + half) % SPACING
        frac = (offset + skip) / SPACING
        frac = jnp.concatenate([frac] * tiers, axis=1)
        values = jnp.concatenate(
            [
                work[b, pl.ds(t, total, stride=tiers), :].astype(jnp.bfloat16)
                for t in range(tiers)
            ],
            axis=1,
        )
        base = (block + 1) // 2 - (first * blocks + 1) // 2
        under = jnp.dot(matrices_ref[base], values, preferred_element_type=jnp.float32)
        over = jnp.dot(matrices_ref[base + 1], values, preferred_element_type=jnp.float32)
        mixed = (1.0 - frac) * under + frac * over
        for t in range(tiers):
            work[b, pl.ds(t, total, stride=tiers), :] = mixed[:, t * LANES : (t + 1) * LANES]
    for p in range(chips):
        for side, out_ref in ((core, keep_ref), (1 - core, give_ref)):
            start = pl.multiple_of((where_ref[p] * 2 + side) * rows, 8)
            for b in range(blocks):
                block = work[b, pl.ds(start, rows), :].reshape(members, tiers, LANES)
                out_ref[p, :, :, b * LANES : (b + 1) * LANES] = block.astype(jnp.bfloat16)


def transform(first, where, pieces, other, matrices):
    chips, members, tiers, cells = other.shape
    out = jax.ShapeDtypeStruct(other.shape, jnp.bfloat16)
    whole = pl.BlockSpec(memory_space=pltpu.VMEM)
    own = pl.BlockSpec((1, members, tiers, cells), lambda i: (i, 0, 0, 0))
    return pl.pallas_call(
        functools.partial(transform_kernel, first, chips),
        grid=(1,),
        in_specs=[pl.BlockSpec(memory_space=pltpu.SMEM)] + [own] * chips + [whole] * 2,
        out_specs=[whole, whole],
        out_shape=[out, out],
        scratch_shapes=[pltpu.VMEM((cells // LANES, chips * 2 * members * tiers, LANES), jnp.float32)],
    )(where, *pieces, other, matrices)


def local_products(window, records, radius_cells, coarse):
    values = window.astype(jnp.float32)
    centre = jnp.mean(values, axis=0)
    departure = values - centre[None, :]
    innovation = records[3] * (records[0] - centre)
    distance = (records[2][None, :] - coarse[:, None]) / radius_cells
    root_weight = jnp.sqrt(jnp.exp(-0.5 * distance * distance) * records[1][None, :])
    scaled = (departure[None, :, :] * root_weight[:, None, :]).astype(jnp.bfloat16)
    weighted = (root_weight * innovation[None, :]).astype(jnp.bfloat16)
    gram_matrix = jnp.einsum("cjo,cmo->cjm", scaled, scaled, preferred_element_type=jnp.float32)
    right_side = jnp.einsum("cjo,co->cj", scaled, weighted, preferred_element_type=jnp.float32)
    return (gram_matrix, right_side)


def ensemble_weights(gram_matrix, right_side):
    sample_runs = gram_matrix.shape[-1]
    identity = jnp.eye(sample_runs, dtype=jnp.float32)
    shifted = gram_matrix + (sample_runs - 1) / inflation * identity[None]
    frobenius = jnp.sqrt(jnp.sum(shifted * shifted, axis=(1, 2)))
    iterate = shifted / frobenius[:, None, None]
    inverse = 1.5 * identity[None] - 0.5 * iterate
    high = lax.Precision.HIGHEST
    iterate = jnp.matmul(iterate, inverse, precision=high)
    for turn in range(1, NS_ITERS):
        factor = 1.5 * identity[None] - 0.5 * jnp.matmul(inverse, iterate, precision=high)
        if turn < NS_ITERS - 1:
            iterate = jnp.matmul(iterate, factor, precision=high)
        inverse = jnp.matmul(factor, inverse, precision=high)
    spread = inverse * jnp.sqrt((sample_runs - 1.0) / frobenius)[:, None, None]
    inner_step = jnp.einsum("cjm,cm->cj", inverse, right_side, precision=high)
    centre = jnp.einsum("cjm,cm->cj", inverse, inner_step, precision=high) / frobenius[:, None]
    weights = spread + centre[:, :, None]
    weights = weights - jnp.mean(weights, axis=1, keepdims=True) + 1.0 / sample_runs
    return jnp.swapaxes(weights, 1, 2).astype(jnp.bfloat16)


def moves(regions):
    across = regions // 8
    return [(dz, dx) for dz in (3, 2, 1, 0) for dx in reversed(range(across))]


def spread(block):
    return lax.all_to_all(block, "region", split_axis=0, concat_axis=0, tiled=True)


def analyse(
    prior_samples, measured_site, measured_datum, inverse_variance, active_slots, cutoff_distance
):
    members, tiers, _ = prior_samples.shape
    regions = lax.axis_size("region")
    levels = lax.axis_size("level")
    grid_sites = COARSE * SPACING
    slots = measured_site.shape[0]
    me = lax.axis_index("region")
    tier_rank = lax.axis_index("level")
    chips = regions // 2
    across = chips // 4
    core = me % 2
    chip = me // 2
    steps = moves(regions)

    def target(chip_index, dz, dx):
        return ((chip_index // across) ^ dz) * across + ((chip_index % across) ^ dx)

    def swap(block, rank):
        dz, dx = steps[rank]
        if (dz, dx) == (0, 0):
            return block
        pairs = [(i, target(i // 2, dz, dx) * 2 + i % 2) for i in range(regions)]
        return lax.ppermute(block, "region", pairs)

    def swap_core(block):
        return lax.ppermute(block, "region", [(i, i ^ 1) for i in range(regions)])

    partners = [target(chip, dz, dx) for dz, dx in steps]
    where = jnp.stack(partners + [core]).astype(jnp.int32)

    live = jnp.arange(slots, dtype=jnp.int32) < active_slots[0]
    live_f = live.astype(jnp.float32)
    records = jnp.stack(
        [
            jnp.where(live, measured_site, -1).astype(jnp.float32),
            measured_datum,
            inverse_variance * live_f,
        ]
    )
    table = spread(jnp.broadcast_to(records[None], (regions,) + records.shape))
    sites = table[:, 0:1].astype(jnp.int32)
    cell = jnp.where(sites < 0, -1, sites % grid_sites)
    tier = jnp.where(sites < 0, -1, sites // grid_sites - tier_rank * tiers)
    observed = gather_observed(prior_samples, cell, tier)
    flip = [(i, (i + 1) % levels) for i in range(levels)]
    observed = observed + lax.ppermute(observed, "level", flip)
    observed = spread(observed)
    observed = observed.reshape(regions * members, slots)
    up = [(i, (i + 1) % regions) for i in range(regions)]
    down = [(target_, source) for source, target_ in up]
    window = jnp.concatenate(
        [lax.ppermute(observed, "region", up), observed, lax.ppermute(observed, "region", down)],
        axis=1,
    )
    near = []
    for shift in (-1, 0, 1):
        row = lax.dynamic_index_in_dim(table, (me + shift) % regions, axis=0, keepdims=False)
        site = row[0].astype(jnp.int32)
        here = (site >= 0).astype(jnp.float32)
        point = jnp.where(site < 0, 0, site % grid_sites).astype(jnp.float32)
        near.append(jnp.stack([row[1], row[2], point + shift * grid_sites, here]))
    near = jnp.concatenate(near, axis=1)
    share = COARSE // levels
    coarse = (
        SPACING // 2 + SPACING * (tier_rank * share + jnp.arange(share, dtype=jnp.int32))
    ).astype(jnp.float32)
    gram_matrix, right_side = local_products(
        window, near, cutoff_distance[0].astype(jnp.float32), coarse
    )
    weights = ensemble_weights(gram_matrix, right_side)
    opposite = lax.ppermute(weights, "level", flip)
    weights = jnp.where(
        tier_rank == 0,
        jnp.concatenate([weights, opposite]),
        jnp.concatenate([opposite, weights]),
    )
    before = lax.ppermute(weights[-1:], "region", up)
    beyond = lax.ppermute(weights[:1], "region", down)

    analysis = None
    for half in range(HALVES):
        pieces = cut(half, where, prior_samples)
        pieces = [swap(block, rank) for rank, block in enumerate(pieces)]
        other = hand(where, pieces)
        other = swap_core(other)
        if half == 0:
            matrices = jnp.concatenate([before, weights[: COARSE // 2 + 1]])
        else:
            matrices = jnp.concatenate([weights[COARSE // 2 - 1 :], beyond])
        keep, give = transform(half, where, pieces, other, matrices)
        got = swap_core(give)
        blocks = pack(where, keep, got)
        blocks = [swap(block, rank) for rank, block in enumerate(blocks)]
        analysis = join(half, where, blocks, prior_samples.shape, analysis)
    return analysis


def solution(mesh):
    return jax.shard_map(
        analyse,
        mesh=mesh,
        in_specs=(
            P("region", "level", None),
            P("region"),
            P("region"),
            P("region"),
            P("region"),
            P("region"),
        ),
        out_specs=P("region", "level", None),
        check_vma=False,
    )
```

```python
import functools

import jax
import jax.numpy as jnp
from jax import lax
from jax.experimental import pallas as pl
from jax.experimental.pallas import tpu as pltpu
from jax.sharding import PartitionSpec as P


COARSE = 6
SPACING = 256
NS_ITERS = 5
HALVES = 2
LANES = 128

inflation = 1.1


def gather_kernel(cell_ref, level_ref, fields_ref, out_ref):
    members, tiers, cells = fields_ref.shape
    slots = cell_ref.shape[-1]
    rows = lax.broadcasted_iota(jnp.int32, (cells, slots), 0)
    chosen = jnp.where(rows == cell_ref[0], 1.0, 0.0).astype(jnp.bfloat16)
    fields = fields_ref[...].reshape(members * tiers, cells)
    found = jnp.dot(fields, chosen, preferred_element_type=jnp.float32)
    found = found.reshape(members, tiers, slots)
    tier = lax.broadcasted_iota(jnp.int32, (members, tiers, slots), 1)
    found = jnp.where(tier == level_ref[...], found, 0.0)
    out_ref[0] = jnp.sum(found, axis=1).astype(jnp.bfloat16)


def gather_observed(prior, cell, level):
    members, tiers, total = prior.shape
    regions, _, slots = cell.shape
    cells = total // regions
    return pl.pallas_call(
        gather_kernel,
        grid=(regions,),
        in_specs=[
            pl.BlockSpec((1, 1, slots), lambda r: (r, 0, 0)),
            pl.BlockSpec((1, 1, slots), lambda r: (r, 0, 0)),
            pl.BlockSpec((members, tiers, cells), lambda r: (0, 0, r)),
        ],
        out_specs=pl.BlockSpec((1, members, slots), lambda r: (r, 0, 0)),
        out_shape=jax.ShapeDtypeStruct((regions, members, slots), jnp.bfloat16),
        name="gather_observed",
    )(cell, level, prior)


def copy_all(reads, writes, arrived, left):
    share = len(reads) // len(writes)
    into = [pltpu.make_async_copy(a, b, arrived.at[i]) for i, (a, b) in enumerate(reads)]
    onward = [pltpu.make_async_copy(a, b, left.at[i]) for i, (a, b) in enumerate(writes)]
    for copy in into:
        copy.start()
    if share:
        for i, copy in enumerate(onward):
            for part in into[i * share : (i + 1) * share]:
                part.wait()
            copy.start()
    else:
        share = len(writes) // len(reads)
        for i, copy in enumerate(into):
            copy.wait()
            for part in onward[i * share : (i + 1) * share]:
                part.start()
    for copy in onward:
        copy.wait()


def moved(kernel, where, operands, out_shape, block, count, aliases=None):
    anywhere = pl.BlockSpec(memory_space=pl.ANY)
    several = isinstance(out_shape, list)
    return pl.pallas_call(
        kernel,
        in_specs=[pl.BlockSpec(memory_space=pltpu.SMEM)] + [anywhere] * len(operands),
        out_specs=[anywhere] * len(out_shape) if several else anywhere,
        out_shape=out_shape,
        scratch_shapes=[
            pltpu.VMEM((count,) + block, jnp.bfloat16),
            pltpu.SemaphoreType.DMA((2 * count,)),
            pltpu.SemaphoreType.DMA((2 * count,)),
        ],
        input_output_aliases=aliases or {},
    )(where, *operands)


def spans(half, cells):
    shift = SPACING // 2
    if half < HALVES - 1:
        return [(0, half * cells + shift, cells)]
    return [(0, half * cells + shift, cells - shift), (cells - shift, 0, shift)]


def cell_spans(where_ref, rank, side, half, cells):
    chips = where_ref.shape[0] - 1
    core = where_ref[chips]
    region = where_ref[rank] * 2 + (core if side == 0 else 1 - core)
    for lane, cell, count in spans(half, cells):
        first = pl.multiple_of(region * (HALVES * cells) + cell, LANES)
        yield pl.ds(lane, count), pl.ds(first, count)


def cut(half, where, prior, ranks):
    chips = where.shape[0] - 1
    members, tiers, total = prior.shape
    cells = total // (2 * chips * HALVES)
    shape = jax.ShapeDtypeStruct((2, members, tiers, cells), prior.dtype)

    def kernel(where_ref, prior_ref, *refs):
        reads, writes = [], []
        stage, arrived, left = refs[len(ranks) :]
        for i, rank in enumerate(ranks):
            for side in range(2):
                slot = stage.at[2 * i + side]
                for lanes, source in cell_spans(where_ref, rank, side, half, cells):
                    reads.append((prior_ref.at[:, :, source], slot.at[:, :, lanes]))
                writes.append((slot, refs[i].at[side]))
        copy_all(reads, writes, arrived, left)

    return moved(kernel, where, [prior], [shape] * len(ranks), shape.shape[1:], 2 * len(ranks))


def hand(where, pieces):
    chips = len(pieces)
    shape = jax.ShapeDtypeStruct((chips,) + pieces[0].shape[1:], pieces[0].dtype)

    def kernel(where_ref, *refs):
        out_ref, stage, arrived, left = refs[chips:]
        copy_all(
            [(refs[p].at[1], stage.at[p]) for p in range(chips)],
            [(stage.at[p], out_ref.at[p]) for p in range(chips)],
            arrived,
            left,
        )

    return moved(kernel, where, pieces, shape, shape.shape[1:], chips)


def pack(where, keep, got):
    chips = keep.shape[0]
    shape = jax.ShapeDtypeStruct((2,) + keep.shape[1:], keep.dtype)

    def kernel(where_ref, keep_ref, got_ref, *refs):
        stage, arrived, left = refs[chips:]
        reads, writes = [], []
        for p in range(chips):
            for side, source in enumerate((keep_ref, got_ref)):
                slot = stage.at[2 * p + side]
                reads.append((source.at[p], slot))
                writes.append((slot, refs[p].at[side]))
        copy_all(reads, writes, arrived, left)

    return moved(kernel, where, [keep, got], [shape] * chips, shape.shape[1:], 2 * chips)


def join(half, where, blocks, shape, base, ranks):
    cells = blocks[0].shape[-1]
    operands = [blocks[rank] for rank in ranks] + ([] if base is None else [base])

    def kernel(where_ref, *refs):
        out_ref, stage, arrived, left = refs[len(operands) :]
        reads, writes = [], []
        for i, rank in enumerate(ranks):
            for side in range(2):
                slot = stage.at[2 * i + side]
                reads.append((refs[i].at[side], slot))
                for lanes, target in cell_spans(where_ref, rank, side, half, cells):
                    writes.append((slot.at[:, :, lanes], out_ref.at[:, :, target]))
        copy_all(reads, writes, arrived, left)

    aliases = None if base is None else {len(operands): 0}
    out = jax.ShapeDtypeStruct(shape, blocks[0].dtype)
    return moved(kernel, where, operands, out, blocks[0].shape[1:], 2 * len(ranks), aliases)


def transform_kernel(first, chips, where_ref, *refs):
    pieces = refs[:chips]
    other_ref, matrices_ref, keep_ref, give_ref, work = refs[chips:]
    _, members, tiers, cells = other_ref.shape
    total = chips * 2 * members
    rows = members * tiers
    core = where_ref[chips]
    for p in range(chips):
        for side, piece in ((core, pieces[p][0]), (1 - core, other_ref[p])):
            start = pl.multiple_of((where_ref[p] * 2 + side) * rows, 8)
            piece = piece.astype(jnp.float32).reshape(rows, cells)
            for b in range(cells // LANES):
                work[b, pl.ds(start, rows), :] = piece[:, b * LANES : (b + 1) * LANES]
    offset = lax.broadcasted_iota(jnp.int32, (1, LANES), 1).astype(jnp.float32)
    half = SPACING // 2
    blocks = cells // LANES
    for b in range(blocks):
        block = (first * blocks + b + half // LANES) % (HALVES * blocks)
        skip = (block * LANES + half) % SPACING
        frac = (offset + skip) / SPACING
        frac = jnp.concatenate([frac] * tiers, axis=1)
        values = jnp.concatenate(
            [
                work[b, pl.ds(t, total, stride=tiers), :].astype(jnp.bfloat16)
                for t in range(tiers)
            ],
            axis=1,
        )
        base = (block * LANES + half) // SPACING - (first < HALVES - 1)
        under = jnp.dot(matrices_ref[base], values, preferred_element_type=jnp.float32)
        over = jnp.dot(matrices_ref[base + 1], values, preferred_element_type=jnp.float32)
        mixed = (1.0 - frac) * under + frac * over
        for t in range(tiers):
            work[b, pl.ds(t, total, stride=tiers), :] = mixed[:, t * LANES : (t + 1) * LANES]
    for p in range(chips):
        for side, out_ref in ((core, keep_ref), (1 - core, give_ref)):
            start = pl.multiple_of((where_ref[p] * 2 + side) * rows, 8)
            for b in range(blocks):
                block = work[b, pl.ds(start, rows), :].reshape(members, tiers, LANES)
                out_ref[p, :, :, b * LANES : (b + 1) * LANES] = block.astype(jnp.bfloat16)


def transform(first, where, pieces, other, matrices):
    chips, members, tiers, cells = other.shape
    out = jax.ShapeDtypeStruct(other.shape, jnp.bfloat16)
    whole = pl.BlockSpec(memory_space=pltpu.VMEM)
    own = pl.BlockSpec((1, members, tiers, cells), lambda i: (i, 0, 0, 0))
    return pl.pallas_call(
        functools.partial(transform_kernel, first, chips),
        grid=(1,),
        in_specs=[pl.BlockSpec(memory_space=pltpu.SMEM)] + [own] * chips + [whole] * 2,
        out_specs=[whole, whole],
        out_shape=[out, out],
        scratch_shapes=[pltpu.VMEM((cells // LANES, chips * 2 * members * tiers, LANES), jnp.float32)],
    )(where, *pieces, other, matrices)


def local_products(window, records, radius_cells, coarse):
    values = window.astype(jnp.float32)
    centre = jnp.mean(values, axis=0)
    departure = values - centre[None, :]
    innovation = records[3] * (records[0] - centre)
    distance = (records[2][None, :] - coarse[:, None]) / radius_cells
    root_weight = jnp.sqrt(jnp.exp(-0.5 * distance * distance) * records[1][None, :])
    scaled = (departure[None, :, :] * root_weight[:, None, :]).astype(jnp.bfloat16)
    weighted = (root_weight * innovation[None, :]).astype(jnp.bfloat16)
    gram_matrix = jnp.einsum("cjo,cmo->cjm", scaled, scaled, preferred_element_type=jnp.float32)
    right_side = jnp.einsum("cjo,co->cj", scaled, weighted, preferred_element_type=jnp.float32)
    return (gram_matrix, right_side)


def ensemble_weights(gram_matrix, right_side):
    sample_runs = gram_matrix.shape[-1]
    identity = jnp.eye(sample_runs, dtype=jnp.float32)
    shifted = gram_matrix + (sample_runs - 1) / inflation * identity[None]
    frobenius = jnp.sqrt(jnp.sum(shifted * shifted, axis=(1, 2)))
    iterate = shifted / frobenius[:, None, None]
    inverse = 1.5 * identity[None] - 0.5 * iterate
    high = lax.Precision.HIGHEST
    iterate = jnp.matmul(iterate, inverse, precision=high)
    for turn in range(1, NS_ITERS):
        factor = 1.5 * identity[None] - 0.5 * jnp.matmul(inverse, iterate, precision=high)
        if turn < NS_ITERS - 1:
            iterate = jnp.matmul(iterate, factor, precision=high)
        inverse = jnp.matmul(factor, inverse, precision=high)
    spread = inverse * jnp.sqrt((sample_runs - 1.0) / frobenius)[:, None, None]
    inner_step = jnp.einsum("cjm,cm->cj", inverse, right_side, precision=high)
    centre = jnp.einsum("cjm,cm->cj", inverse, inner_step, precision=high) / frobenius[:, None]
    weights = spread + centre[:, :, None]
    weights = weights - jnp.mean(weights, axis=1, keepdims=True) + 1.0 / sample_runs
    return jnp.swapaxes(weights, 1, 2).astype(jnp.bfloat16)


def moves(regions):
    across = regions // 8
    return [(dz, dx) for dz in (3, 2, 1, 0) for dx in reversed(range(across))]


def spread(block):
    return lax.all_to_all(block, "region", split_axis=0, concat_axis=0, tiled=True)


def analyse(
    prior_samples, measured_site, measured_datum, inverse_variance, active_slots, cutoff_distance
):
    members, tiers, _ = prior_samples.shape
    regions = lax.axis_size("region")
    levels = lax.axis_size("level")
    grid_sites = COARSE * SPACING
    slots = measured_site.shape[0]
    me = lax.axis_index("region")
    tier_rank = lax.axis_index("level")
    chips = regions // 2
    across = chips // 4
    core = me % 2
    chip = me // 2
    steps = moves(regions)

    def target(chip_index, dz, dx):
        return ((chip_index // across) ^ dz) * across + ((chip_index % across) ^ dx)

    def swap(block, rank):
        dz, dx = steps[rank]
        if (dz, dx) == (0, 0):
            return block
        pairs = [(i, target(i // 2, dz, dx) * 2 + i % 2) for i in range(regions)]
        return lax.ppermute(block, "region", pairs)

    def swap_core(block):
        return lax.ppermute(block, "region", [(i, i ^ 1) for i in range(regions)])

    partners = [target(chip, dz, dx) for dz, dx in steps]
    where = jnp.stack(partners + [core]).astype(jnp.int32)

    live = jnp.arange(slots, dtype=jnp.int32) < active_slots[0]
    live_f = live.astype(jnp.float32)
    records = jnp.stack(
        [
            jnp.where(live, measured_site, -1).astype(jnp.float32),
            measured_datum,
            inverse_variance * live_f,
        ]
    )
    table = spread(jnp.broadcast_to(records[None], (regions,) + records.shape))
    sites = table[:, 0:1].astype(jnp.int32)
    cell = jnp.where(sites < 0, -1, sites % grid_sites)
    tier = jnp.where(sites < 0, -1, sites // grid_sites - tier_rank * tiers)
    observed = gather_observed(prior_samples, cell, tier)
    flip = [(i, (i + 1) % levels) for i in range(levels)]
    observed = observed + lax.ppermute(observed, "level", flip)
    observed = spread(observed)
    observed = observed.reshape(regions * members, slots)
    up = [(i, (i + 1) % regions) for i in range(regions)]
    down = [(target_, source) for source, target_ in up]
    window = jnp.concatenate(
        [lax.ppermute(observed, "region", up), observed, lax.ppermute(observed, "region", down)],
        axis=1,
    )
    near = []
    for shift in (-1, 0, 1):
        row = lax.dynamic_index_in_dim(table, (me + shift) % regions, axis=0, keepdims=False)
        site = row[0].astype(jnp.int32)
        here = (site >= 0).astype(jnp.float32)
        point = jnp.where(site < 0, 0, site % grid_sites).astype(jnp.float32)
        near.append(jnp.stack([row[1], row[2], point + shift * grid_sites, here]))
    near = jnp.concatenate(near, axis=1)
    share = COARSE // levels
    coarse = (
        SPACING // 2 + SPACING * (tier_rank * share + jnp.arange(share, dtype=jnp.int32))
    ).astype(jnp.float32)
    gram_matrix, right_side = local_products(
        window, near, cutoff_distance[0].astype(jnp.float32), coarse
    )
    weights = ensemble_weights(gram_matrix, right_side)
    opposite = lax.ppermute(weights, "level", flip)
    weights = jnp.where(
        tier_rank == 0,
        jnp.concatenate([weights, opposite]),
        jnp.concatenate([opposite, weights]),
    )
    before = lax.ppermute(weights[-1:], "region", up)
    beyond = lax.ppermute(weights[:1], "region", down)

    analysis = None
    for half in range(HALVES):
        early = -(-2 * (chips - 1) // 7) if half == 0 else 0
        pieces = []
        if early:
            pieces += cut(half, where, prior_samples, range(early))
        pieces += cut(half, where, prior_samples, range(early, chips))
        pieces = [swap(block, rank) for rank, block in enumerate(pieces)]
        other = hand(where, pieces)
        other = swap_core(other)
        matrices = weights
        if half == HALVES - 1:
            matrices = jnp.concatenate([before, weights, beyond])
        keep, give = transform(half, where, pieces, other, matrices)
        got = swap_core(give)
        blocks = pack(where, keep, got)
        blocks = [swap(block, rank) for rank, block in enumerate(blocks)]
        late = [] if half == 0 else list(range(across, 2 * across))
        rest = [rank for rank in range(chips) if rank not in late]
        shape = prior_samples.shape
        analysis = join(half, where, blocks, shape, analysis, rest)
        if late:
            analysis = join(half, where, blocks, shape, analysis, late)
    return analysis


def solution(mesh):
    return jax.shard_map(
        analyse,
        mesh=mesh,
        in_specs=(
            P("region", "level", None),
            P("region"),
            P("region"),
            P("region"),
            P("region"),
            P("region"),
        ),
        out_specs=P("region", "level", None),
        check_vma=False,
    )
```

```python
import functools

import jax
import jax.numpy as jnp
from jax import lax
from jax.experimental import pallas as pl
from jax.experimental.pallas import tpu as pltpu
from jax.sharding import PartitionSpec as P


COARSE = 6
SPACING = 256
NS_ITERS = 5
HALVES = 2
LANES = 128

inflation = 1.1


def moves(regions):
    across = regions // 8
    steps = [(dz, dx) for dz in (3, 2, 1, 0) for dx in reversed(range(across))]
    turns = zip(steps[: 2 * across], steps[2 * across :])
    return [step for turn in turns for step in turn]


def target(chip, step, across):
    dz, dx = step
    return ((chip // across) ^ dz) * across + ((chip % across) ^ dx)


def standing(regions):
    across = regions // 8
    me = lax.axis_index("region")
    core = lax.rem(me, 2)
    row, column = lax.div(me, 2 * across), lax.rem(lax.div(me, 2), across)
    return core, [(row ^ dz) * across + (column ^ dx) for dz, dx in moves(regions)]


def gather_kernel(cell_ref, level_ref, fields_ref, out_ref):
    members, tiers, cells = fields_ref.shape
    slots = cell_ref.shape[-1]
    rows = lax.broadcasted_iota(jnp.int32, (cells, slots), 0)
    chosen = jnp.where(rows == cell_ref[0], 1.0, 0.0).astype(jnp.bfloat16)
    fields = fields_ref[...].reshape(members * tiers, cells)
    found = jnp.dot(fields, chosen, preferred_element_type=jnp.float32)
    found = found.reshape(members, tiers, slots)
    tier = lax.broadcasted_iota(jnp.int32, (members, tiers, slots), 1)
    found = jnp.where(tier == level_ref[...], found, 0.0)
    out_ref[0] = jnp.sum(found, axis=1).astype(jnp.bfloat16)


def gather_observed(prior, cell, level):
    members, tiers, total = prior.shape
    regions, _, slots = cell.shape
    cells = total // regions
    return pl.pallas_call(
        gather_kernel,
        grid=(regions,),
        in_specs=[
            pl.BlockSpec((1, 1, slots), lambda r: (r, 0, 0)),
            pl.BlockSpec((1, 1, slots), lambda r: (r, 0, 0)),
            pl.BlockSpec((members, tiers, cells), lambda r: (0, 0, r)),
        ],
        out_specs=pl.BlockSpec((1, members, slots), lambda r: (r, 0, 0)),
        out_shape=jax.ShapeDtypeStruct((regions, members, slots), jnp.bfloat16),
        name="gather_observed",
    )(cell, level, prior)


def copy_all(reads, writes, arrived, left):
    share = len(reads) // len(writes)
    into = [pltpu.make_async_copy(a, b, arrived.at[i]) for i, (a, b) in enumerate(reads)]
    onward = [pltpu.make_async_copy(a, b, left.at[i]) for i, (a, b) in enumerate(writes)]
    for copy in into:
        copy.start()
    if share:
        for i, copy in enumerate(onward):
            for part in into[i * share : (i + 1) * share]:
                part.wait()
            copy.start()
    else:
        share = len(writes) // len(reads)
        for i, copy in enumerate(into):
            copy.wait()
            for part in onward[i * share : (i + 1) * share]:
                part.start()
    for copy in onward:
        copy.wait()


def moved(kernel, operands, out_shape, block, count, aliases=None):
    anywhere = pl.BlockSpec(memory_space=pl.ANY)
    several = isinstance(out_shape, list)
    return pl.pallas_call(
        kernel,
        in_specs=[anywhere] * len(operands),
        out_specs=[anywhere] * len(out_shape) if several else anywhere,
        out_shape=out_shape,
        scratch_shapes=[
            pltpu.VMEM((count,) + block, jnp.bfloat16),
            pltpu.SemaphoreType.DMA((2 * count,)),
            pltpu.SemaphoreType.DMA((2 * count,)),
        ],
        input_output_aliases=aliases or {},
    )(*operands)


def spans(half, cells):
    shift = SPACING // 2
    if half < HALVES - 1:
        return [(0, half * cells + shift, cells)]
    return [(0, half * cells + shift, cells - shift), (cells - shift, 0, shift)]


def cell_spans(chip, core, half, cells):
    region = chip * 2 + core
    for lane, cell, count in spans(half, cells):
        first = pl.multiple_of(region * (HALVES * cells) + cell, LANES)
        yield pl.ds(lane, count), pl.ds(first, count)


def cut(half, prior, ranks, regions):
    members, tiers, total = prior.shape
    cells = total // (regions * HALVES)
    shape = jax.ShapeDtypeStruct((2, members, tiers, cells), prior.dtype)

    def kernel(prior_ref, *refs):
        core, partners = standing(regions)
        reads, writes = [], []
        stage, arrived, left = refs[len(ranks) :]
        for i, rank in enumerate(ranks):
            for side in range(2):
                slot = stage.at[2 * i + side]
                for lanes, source in cell_spans(partners[rank], core ^ side, half, cells):
                    reads.append((prior_ref.at[:, :, source], slot.at[:, :, lanes]))
                writes.append((slot, refs[i].at[side]))
        copy_all(reads, writes, arrived, left)

    return moved(kernel, [prior], [shape] * len(ranks), shape.shape[1:], 2 * len(ranks))


def hand(pieces):
    chips = len(pieces)
    shape = jax.ShapeDtypeStruct((chips,) + pieces[0].shape[1:], pieces[0].dtype)

    def kernel(*refs):
        out_ref, stage, arrived, left = refs[chips:]
        copy_all(
            [(refs[p].at[1], stage.at[p]) for p in range(chips)],
            [(stage.at[p], out_ref.at[p]) for p in range(chips)],
            arrived,
            left,
        )

    return moved(kernel, pieces, shape, shape.shape[1:], chips)


def pack(keep, got):
    chips = keep.shape[0]
    shape = jax.ShapeDtypeStruct((2,) + keep.shape[1:], keep.dtype)

    def kernel(keep_ref, got_ref, *refs):
        stage, arrived, left = refs[chips:]
        reads, writes = [], []
        for p in range(chips):
            for side, source in enumerate((keep_ref, got_ref)):
                slot = stage.at[2 * p + side]
                reads.append((source.at[p], slot))
                writes.append((slot, refs[p].at[side]))
        copy_all(reads, writes, arrived, left)

    return moved(kernel, [keep, got], [shape] * chips, shape.shape[1:], 2 * chips)


def join(half, blocks, shape, base, ranks, regions):
    cells = blocks[0].shape[-1]
    operands = [blocks[rank] for rank in ranks] + ([] if base is None else [base])

    def kernel(*refs):
        core, partners = standing(regions)
        out_ref, stage, arrived, left = refs[len(operands) :]
        reads, writes = [], []
        for i, rank in enumerate(ranks):
            for side in range(2):
                slot = stage.at[2 * i + side]
                reads.append((refs[i].at[side], slot))
                for lanes, target in cell_spans(partners[rank], core ^ side, half, cells):
                    writes.append((slot.at[:, :, lanes], out_ref.at[:, :, target]))
        copy_all(reads, writes, arrived, left)

    aliases = None if base is None else {len(operands) - 1: 0}
    out = jax.ShapeDtypeStruct(shape, blocks[0].dtype)
    return moved(kernel, operands, out, blocks[0].shape[1:], 2 * len(ranks), aliases)


def transform_kernel(first, chips, *refs):
    pieces = refs[:chips]
    other_ref, own_ref, opposite_ref, *edges = refs[chips:-4]
    keep_ref, give_ref, work, matrices = refs[-4:]
    core, partners = standing(2 * chips)
    share = own_ref.shape[0]
    rank = lax.axis_index("level")
    for k in range(share):
        matrices[1 + rank * share + k] = own_ref[k]
        matrices[1 + (1 - rank) * share + k] = opposite_ref[k]
    for k, edge in zip((0, 2 * share + 1), edges):
        matrices[k] = edge[0]
    _, members, tiers, cells = other_ref.shape
    total = chips * 2 * members
    rows = members * tiers
    for p in range(chips):
        for side, piece in ((core, pieces[p][0]), (1 - core, other_ref[p])):
            start = pl.multiple_of((partners[p] * 2 + side) * rows, 8)
            piece = piece.astype(jnp.float32).reshape(rows, cells)
            for b in range(cells // LANES):
                work[b, pl.ds(start, rows), :] = piece[:, b * LANES : (b + 1) * LANES]
    offset = lax.broadcasted_iota(jnp.int32, (1, LANES), 1).astype(jnp.float32)
    half = SPACING // 2
    blocks = cells // LANES
    for b in range(blocks):
        block = (first * blocks + b + half // LANES) % (HALVES * blocks)
        skip = (block * LANES + half) % SPACING
        frac = (offset + skip) / SPACING
        frac = jnp.concatenate([frac] * tiers, axis=1)
        values = jnp.concatenate(
            [
                work[b, pl.ds(t, total, stride=tiers), :].astype(jnp.bfloat16)
                for t in range(tiers)
            ],
            axis=1,
        )
        base = (block * LANES + half) // SPACING
        under = jnp.dot(matrices[base], values, preferred_element_type=jnp.float32)
        over = jnp.dot(matrices[base + 1], values, preferred_element_type=jnp.float32)
        mixed = (1.0 - frac) * under + frac * over
        for t in range(tiers):
            work[b, pl.ds(t, total, stride=tiers), :] = mixed[:, t * LANES : (t + 1) * LANES]
    for p in range(chips):
        for side, out_ref in ((core, keep_ref), (1 - core, give_ref)):
            start = pl.multiple_of((partners[p] * 2 + side) * rows, 8)
            for b in range(blocks):
                block = work[b, pl.ds(start, rows), :].reshape(members, tiers, LANES)
                out_ref[p, :, :, b * LANES : (b + 1) * LANES] = block.astype(jnp.bfloat16)


def transform(first, pieces, other, own, opposite, edges):
    chips, members, tiers, cells = other.shape
    out = jax.ShapeDtypeStruct(other.shape, jnp.bfloat16)
    whole = pl.BlockSpec(memory_space=pltpu.VMEM)
    mine = pl.BlockSpec((1, members, tiers, cells), lambda i: (i, 0, 0, 0))
    return pl.pallas_call(
        functools.partial(transform_kernel, first, chips),
        grid=(1,),
        in_specs=[mine] * chips + [whole] * (3 + len(edges)),
        out_specs=[whole, whole],
        out_shape=[out, out],
        scratch_shapes=[
            pltpu.VMEM((cells // LANES, chips * 2 * members * tiers, LANES), jnp.float32),
            pltpu.VMEM((2 * own.shape[0] + 2,) + own.shape[1:], own.dtype),
        ],
    )(*pieces, other, own, opposite, *edges)


def local_products(window, records, radius_cells, coarse):
    values = window.astype(jnp.float32)
    centre = jnp.mean(values, axis=0)
    departure = values - centre[None, :]
    innovation = records[3] * (records[0] - centre)
    distance = (records[2][None, :] - coarse[:, None]) / radius_cells
    root_weight = jnp.sqrt(jnp.exp(-0.5 * distance * distance) * records[1][None, :])
    scaled = (departure[None, :, :] * root_weight[:, None, :]).astype(jnp.bfloat16)
    weighted = (root_weight * innovation[None, :]).astype(jnp.bfloat16)
    gram_matrix = jnp.einsum("cjo,cmo->cjm", scaled, scaled, preferred_element_type=jnp.float32)
    right_side = jnp.einsum("cjo,co->cj", scaled, weighted, preferred_element_type=jnp.float32)
    return (gram_matrix, right_side)


def ensemble_weights(gram_matrix, right_side):
    sample_runs = gram_matrix.shape[-1]
    identity = jnp.eye(sample_runs, dtype=jnp.float32)
    shifted = gram_matrix + (sample_runs - 1) / inflation * identity[None]
    frobenius = jnp.sqrt(jnp.sum(shifted * shifted, axis=(1, 2)))
    iterate = shifted / frobenius[:, None, None]
    inverse = 1.5 * identity[None] - 0.5 * iterate
    high = lax.Precision.HIGH
    iterate = jnp.matmul(iterate, inverse, precision=high)
    for turn in range(1, NS_ITERS):
        factor = 1.5 * identity[None] - 0.5 * jnp.matmul(inverse, iterate, precision=high)
        if turn < NS_ITERS - 1:
            iterate = jnp.matmul(iterate, factor, precision=high)
        inverse = jnp.matmul(factor, inverse, precision=high)
    spread = inverse * jnp.sqrt((sample_runs - 1.0) / frobenius)[:, None, None]
    inner_step = jnp.einsum("cjm,cm->cj", inverse, right_side, precision=high)
    centre = jnp.einsum("cjm,cm->cj", inverse, inner_step, precision=high) / frobenius[:, None]
    weights = spread + centre[:, :, None]
    weights = weights - jnp.mean(weights, axis=1, keepdims=True) + 1.0 / sample_runs
    return jnp.swapaxes(weights, 1, 2).astype(jnp.bfloat16)


def spread(block):
    return lax.all_to_all(block, "region", split_axis=0, concat_axis=0, tiled=True)


def analyse(
    prior_samples, measured_site, measured_datum, inverse_variance, active_slots, cutoff_distance
):
    members, tiers, _ = prior_samples.shape
    regions = lax.axis_size("region")
    levels = lax.axis_size("level")
    grid_sites = COARSE * SPACING
    slots = measured_site.shape[0]
    me = lax.axis_index("region")
    tier_rank = lax.axis_index("level")
    chips = regions // 2
    across = chips // 4
    steps = moves(regions)

    def swap(block, rank):
        if steps[rank] == (0, 0):
            return block
        pairs = [(i, target(i // 2, steps[rank], across) * 2 + i % 2) for i in range(regions)]
        return lax.ppermute(block, "region", pairs)

    def swap_core(block):
        return lax.ppermute(block, "region", [(i, i ^ 1) for i in range(regions)])

    live = jnp.arange(slots, dtype=jnp.int32) < active_slots[0]
    live_f = live.astype(jnp.float32)
    records = jnp.stack(
        [
            jnp.where(live, measured_site, -1).astype(jnp.float32),
            measured_datum,
            inverse_variance * live_f,
        ]
    )
    table = spread(jnp.broadcast_to(records[None], (regions,) + records.shape))
    sites = table[:, 0:1].astype(jnp.int32)
    cell = jnp.where(sites < 0, -1, sites % grid_sites)
    tier = jnp.where(sites < 0, -1, sites // grid_sites - tier_rank * tiers)
    observed = gather_observed(prior_samples, cell, tier)
    flip = [(i, (i + 1) % levels) for i in range(levels)]
    observed = observed + lax.ppermute(observed, "level", flip)
    observed = spread(observed)
    observed = observed.reshape(regions * members, slots)
    up = [(i, (i + 1) % regions) for i in range(regions)]
    down = [(target_, source) for source, target_ in up]
    window = jnp.concatenate(
        [lax.ppermute(observed, "region", up), observed, lax.ppermute(observed, "region", down)],
        axis=1,
    )
    near = []
    for shift in (-1, 0, 1):
        row = lax.dynamic_index_in_dim(table, (me + shift) % regions, axis=0, keepdims=False)
        site = row[0].astype(jnp.int32)
        here = (site >= 0).astype(jnp.float32)
        point = jnp.where(site < 0, 0, site % grid_sites).astype(jnp.float32)
        near.append(jnp.stack([row[1], row[2], point + shift * grid_sites, here]))
    near = jnp.concatenate(near, axis=1)
    share = COARSE // levels
    coarse = (
        SPACING // 2 + SPACING * (tier_rank * share + jnp.arange(share, dtype=jnp.int32))
    ).astype(jnp.float32)
    gram_matrix, right_side = local_products(
        window, near, cutoff_distance[0].astype(jnp.float32), coarse
    )
    weights = ensemble_weights(gram_matrix, right_side)
    opposite = lax.ppermute(weights, "level", flip)
    before = lax.ppermute(jnp.where(tier_rank == 0, opposite, weights)[-1:], "region", up)
    beyond = lax.ppermute(jnp.where(tier_rank == 0, weights, opposite)[:1], "region", down)

    analysis = None
    early_count = -(-2 * (chips - 1) // 7)
    for half in range(HALVES):
        early = -(-(chips - 1) // 7) if half == 0 else 0
        pieces = []
        if early:
            pieces += cut(half, prior_samples, range(early), regions)
        pieces += cut(half, prior_samples, range(early, chips), regions)
        pieces = [swap(block, rank) for rank, block in enumerate(pieces)]
        other = hand(pieces)
        other = swap_core(other)
        edges = [] if half == 0 else [before, beyond]
        keep, give = transform(half, pieces, other, weights, opposite, edges)
        got = swap_core(give)
        blocks = pack(keep, got)
        blocks = [swap(block, rank) for rank, block in enumerate(blocks)]
        late = [] if half == 0 else list(range(chips - 1 - early_count, chips - 1))
        rest = [rank for rank in range(chips) if rank not in late]
        shape = prior_samples.shape
        analysis = join(half, blocks, shape, analysis, rest, regions)
        if late:
            analysis = join(half, blocks, shape, analysis, late, regions)
    return analysis


def solution(mesh):
    return jax.shard_map(
        analyse,
        mesh=mesh,
        in_specs=(
            P("region", "level", None),
            P("region"),
            P("region"),
            P("region"),
            P("region"),
            P("region"),
        ),
        out_specs=P("region", "level", None),
        check_vma=False,
    )
```

```python
import functools

import jax
import jax.numpy as jnp
from jax import lax
from jax.experimental import pallas as pl
from jax.experimental.pallas import tpu as pltpu
from jax.sharding import PartitionSpec as P


COARSE = 6
SPACING = 256
NS_ITERS = 5
HALVES = 2
LANES = 128

inflation = 1.1


def moves(regions):
    across = regions // 8
    steps = [(dz, dx) for dz in (3, 2, 1, 0) for dx in reversed(range(across))]
    turns = zip(steps[: 2 * across], steps[2 * across :])
    return [step for turn in turns for step in turn]


def target(chip, step, across):
    dz, dx = step
    return ((chip // across) ^ dz) * across + ((chip % across) ^ dx)


def standing(regions):
    across = regions // 8
    me = lax.axis_index("region")
    core = lax.rem(me, 2)
    row, column = lax.div(me, 2 * across), lax.rem(lax.div(me, 2), across)
    return core, [(row ^ dz) * across + (column ^ dx) for dz, dx in moves(regions)]


def gather_kernel(cell_ref, level_ref, fields_ref, out_ref):
    members, tiers, cells = fields_ref.shape
    slots = cell_ref.shape[-1]
    rows = lax.broadcasted_iota(jnp.int32, (cells, slots), 0)
    chosen = jnp.where(rows == cell_ref[0], 1.0, 0.0).astype(jnp.bfloat16)
    fields = fields_ref[...].reshape(members * tiers, cells)
    found = jnp.dot(fields, chosen, preferred_element_type=jnp.float32)
    found = found.reshape(members, tiers, slots)
    tier = lax.broadcasted_iota(jnp.int32, (members, tiers, slots), 1)
    found = jnp.where(tier == level_ref[...], found, 0.0)
    found = jnp.sum(found, axis=1).astype(jnp.bfloat16)
    levels, _, _, share = out_ref.shape
    rank = lax.axis_index("level")
    for h in range(levels):
        out_ref[lax.rem(h + rank, levels), 0] = found[:, h * share : (h + 1) * share]


def gather_observed(prior, cell, level, levels):
    members, tiers, total = prior.shape
    regions, _, slots = cell.shape
    cells = total // regions
    return pl.pallas_call(
        gather_kernel,
        grid=(regions,),
        in_specs=[
            pl.BlockSpec((1, 1, slots), lambda r: (r, 0, 0)),
            pl.BlockSpec((1, 1, slots), lambda r: (r, 0, 0)),
            pl.BlockSpec((members, tiers, cells), lambda r: (0, 0, r)),
        ],
        out_specs=pl.BlockSpec((levels, 1, members, slots // levels), lambda r: (0, r, 0, 0)),
        out_shape=jax.ShapeDtypeStruct(
            (levels, regions, members, slots // levels), jnp.bfloat16
        ),
        name="gather_observed",
    )(cell, level, prior)


def copy_all(reads, writes, arrived, left):
    share = len(reads) // len(writes)
    into = [pltpu.make_async_copy(a, b, arrived.at[i]) for i, (a, b) in enumerate(reads)]
    onward = [pltpu.make_async_copy(a, b, left.at[i]) for i, (a, b) in enumerate(writes)]
    for copy in into:
        copy.start()
    if share:
        for i, copy in enumerate(onward):
            for part in into[i * share : (i + 1) * share]:
                part.wait()
            copy.start()
    else:
        share = len(writes) // len(reads)
        for i, copy in enumerate(into):
            copy.wait()
            for part in onward[i * share : (i + 1) * share]:
                part.start()
    for copy in onward:
        copy.wait()


def moved(kernel, operands, out_shape, block, count, aliases=None):
    anywhere = pl.BlockSpec(memory_space=pl.ANY)
    several = isinstance(out_shape, list)
    return pl.pallas_call(
        kernel,
        in_specs=[anywhere] * len(operands),
        out_specs=[anywhere] * len(out_shape) if several else anywhere,
        out_shape=out_shape,
        scratch_shapes=[
            pltpu.VMEM((count,) + block, jnp.bfloat16),
            pltpu.SemaphoreType.DMA((2 * count,)),
            pltpu.SemaphoreType.DMA((2 * count,)),
        ],
        input_output_aliases=aliases or {},
    )(*operands)


def spans(half, cells):
    shift = SPACING // 2
    if half < HALVES - 1:
        return [(0, half * cells + shift, cells)]
    return [(0, half * cells + shift, cells - shift), (cells - shift, 0, shift)]


def cell_spans(chip, core, half, cells):
    region = chip * 2 + core
    for lane, cell, count in spans(half, cells):
        first = pl.multiple_of(region * (HALVES * cells) + cell, LANES)
        yield pl.ds(lane, count), pl.ds(first, count)


def cut(half, prior, ranks, regions):
    members, tiers, total = prior.shape
    cells = total // (regions * HALVES)
    shape = jax.ShapeDtypeStruct((2, members, tiers, cells), prior.dtype)

    def kernel(prior_ref, *refs):
        core, partners = standing(regions)
        reads, writes = [], []
        stage, arrived, left = refs[len(ranks) :]
        for i, rank in enumerate(ranks):
            for side in range(2):
                slot = stage.at[2 * i + side]
                for lanes, source in cell_spans(partners[rank], core ^ side, half, cells):
                    reads.append((prior_ref.at[:, :, source], slot.at[:, :, lanes]))
                writes.append((slot, refs[i].at[side]))
        copy_all(reads, writes, arrived, left)

    return moved(kernel, [prior], [shape] * len(ranks), shape.shape[1:], 2 * len(ranks))


def hand(pieces):
    chips = len(pieces)
    shape = jax.ShapeDtypeStruct((chips,) + pieces[0].shape[1:], pieces[0].dtype)

    def kernel(*refs):
        out_ref, stage, arrived, left = refs[chips:]
        copy_all(
            [(refs[p].at[1], stage.at[p]) for p in range(chips)],
            [(stage.at[p], out_ref.at[p]) for p in range(chips)],
            arrived,
            left,
        )

    return moved(kernel, pieces, shape, shape.shape[1:], chips)


def pack(keep, got):
    chips = keep.shape[0]
    shape = jax.ShapeDtypeStruct((2,) + keep.shape[1:], keep.dtype)

    def kernel(keep_ref, got_ref, *refs):
        stage, arrived, left = refs[chips:]
        reads, writes = [], []
        for p in range(chips):
            for side, source in enumerate((keep_ref, got_ref)):
                slot = stage.at[2 * p + side]
                reads.append((source.at[p], slot))
                writes.append((slot, refs[p].at[side]))
        copy_all(reads, writes, arrived, left)

    return moved(kernel, [keep, got], [shape] * chips, shape.shape[1:], 2 * chips)


def join(half, blocks, shape, base, ranks, regions):
    cells = blocks[0].shape[-1]
    operands = [blocks[rank] for rank in ranks] + ([] if base is None else [base])

    def kernel(*refs):
        core, partners = standing(regions)
        out_ref, stage, arrived, left = refs[len(operands) :]
        reads, writes = [], []
        for i, rank in enumerate(ranks):
            for side in range(2):
                slot = stage.at[2 * i + side]
                reads.append((refs[i].at[side], slot))
                for lanes, target in cell_spans(partners[rank], core ^ side, half, cells):
                    writes.append((slot.at[:, :, lanes], out_ref.at[:, :, target]))
        copy_all(reads, writes, arrived, left)

    aliases = None if base is None else {len(operands) - 1: 0}
    out = jax.ShapeDtypeStruct(shape, blocks[0].dtype)
    return moved(kernel, operands, out, blocks[0].shape[1:], 2 * len(ranks), aliases)


def transform_kernel(first, chips, *refs):
    pieces = refs[:chips]
    other_ref, own_ref, opposite_ref, *edges = refs[chips:-4]
    keep_ref, give_ref, work, matrices = refs[-4:]
    core, partners = standing(2 * chips)
    share = own_ref.shape[0]
    rank = lax.axis_index("level")
    for k in range(share):
        matrices[1 + rank * share + k] = own_ref[k]
        matrices[1 + (1 - rank) * share + k] = opposite_ref[k]
    for k, edge in zip((0, 2 * share + 1), edges):
        matrices[k] = edge[0]
    _, members, tiers, cells = other_ref.shape
    total = chips * 2 * members
    rows = members * tiers
    for p in range(chips):
        for side, piece in ((core, pieces[p][0]), (1 - core, other_ref[p])):
            start = pl.multiple_of((partners[p] * 2 + side) * rows, 8)
            piece = piece.astype(jnp.float32).reshape(rows, cells)
            for b in range(cells // LANES):
                work[b, pl.ds(start, rows), :] = piece[:, b * LANES : (b + 1) * LANES]
    offset = lax.broadcasted_iota(jnp.int32, (1, LANES), 1).astype(jnp.float32)
    half = SPACING // 2
    blocks = cells // LANES
    for b in range(blocks):
        block = (first * blocks + b + half // LANES) % (HALVES * blocks)
        skip = (block * LANES + half) % SPACING
        frac = (offset + skip) / SPACING
        frac = jnp.concatenate([frac] * tiers, axis=1)
        values = jnp.concatenate(
            [
                work[b, pl.ds(t, total, stride=tiers), :].astype(jnp.bfloat16)
                for t in range(tiers)
            ],
            axis=1,
        )
        base = (block * LANES + half) // SPACING
        under = jnp.dot(matrices[base], values, preferred_element_type=jnp.float32)
        over = jnp.dot(matrices[base + 1], values, preferred_element_type=jnp.float32)
        mixed = (1.0 - frac) * under + frac * over
        for t in range(tiers):
            work[b, pl.ds(t, total, stride=tiers), :] = mixed[:, t * LANES : (t + 1) * LANES]
    for p in range(chips):
        for side, out_ref in ((core, keep_ref), (1 - core, give_ref)):
            start = pl.multiple_of((partners[p] * 2 + side) * rows, 8)
            for b in range(blocks):
                block = work[b, pl.ds(start, rows), :].reshape(members, tiers, LANES)
                out_ref[p, :, :, b * LANES : (b + 1) * LANES] = block.astype(jnp.bfloat16)


def transform(first, pieces, other, own, opposite, edges):
    chips, members, tiers, cells = other.shape
    out = jax.ShapeDtypeStruct(other.shape, jnp.bfloat16)
    whole = pl.BlockSpec(memory_space=pltpu.VMEM)
    mine = pl.BlockSpec((1, members, tiers, cells), lambda i: (i, 0, 0, 0))
    return pl.pallas_call(
        functools.partial(transform_kernel, first, chips),
        grid=(1,),
        in_specs=[mine] * chips + [whole] * (3 + len(edges)),
        out_specs=[whole, whole],
        out_shape=[out, out],
        scratch_shapes=[
            pltpu.VMEM((cells // LANES, chips * 2 * members * tiers, LANES), jnp.float32),
            pltpu.VMEM((2 * own.shape[0] + 2,) + own.shape[1:], own.dtype),
        ],
    )(*pieces, other, own, opposite, *edges)


def local_products(window, records, radius_cells, coarse):
    values = window.astype(jnp.float32)
    centre = jnp.mean(values, axis=0)
    departure = values - centre[None, :]
    innovation = records[3] * (records[0] - centre)
    distance = (records[2][None, :] - coarse[:, None]) / radius_cells
    root_weight = jnp.sqrt(jnp.exp(-0.5 * distance * distance) * records[1][None, :])
    scaled = (departure[None, :, :] * root_weight[:, None, :]).astype(jnp.bfloat16)
    weighted = (root_weight * innovation[None, :]).astype(jnp.bfloat16)
    gram_matrix = jnp.einsum("cjo,cmo->cjm", scaled, scaled, preferred_element_type=jnp.float32)
    right_side = jnp.einsum("cjo,co->cj", scaled, weighted, preferred_element_type=jnp.float32)
    return (gram_matrix, right_side)


def ensemble_weights(gram_matrix, right_side):
    sample_runs = gram_matrix.shape[-1]
    identity = jnp.eye(sample_runs, dtype=jnp.float32)
    shifted = gram_matrix + (sample_runs - 1) / inflation * identity[None]
    frobenius = jnp.sqrt(jnp.sum(shifted * shifted, axis=(1, 2)))
    iterate = shifted / frobenius[:, None, None]
    inverse = 1.5 * identity[None] - 0.5 * iterate
    high = lax.Precision.HIGHEST
    iterate = jnp.matmul(iterate, inverse, precision=high)
    for turn in range(1, NS_ITERS):
        factor = 1.5 * identity[None] - 0.5 * jnp.matmul(inverse, iterate, precision=high)
        if turn < NS_ITERS - 1:
            iterate = jnp.matmul(iterate, factor, precision=high)
        inverse = jnp.matmul(factor, inverse, precision=high)
    spread = inverse * jnp.sqrt((sample_runs - 1.0) / frobenius)[:, None, None]
    inner_step = jnp.einsum("cjm,cm->cj", inverse, right_side, precision=high)
    centre = jnp.einsum("cjm,cm->cj", inverse, inner_step, precision=high) / frobenius[:, None]
    weights = spread + centre[:, :, None]
    weights = weights - jnp.mean(weights, axis=1, keepdims=True) + 1.0 / sample_runs
    return jnp.swapaxes(weights, 1, 2).astype(jnp.bfloat16)


def spread(block):
    return lax.all_to_all(block, "region", split_axis=0, concat_axis=0, tiled=True)


def analyse(
    prior_samples, measured_site, measured_datum, inverse_variance, active_slots, cutoff_distance
):
    members, tiers, _ = prior_samples.shape
    regions = lax.axis_size("region")
    levels = lax.axis_size("level")
    grid_sites = COARSE * SPACING
    slots = measured_site.shape[0]
    me = lax.axis_index("region")
    tier_rank = lax.axis_index("level")
    chips = regions // 2
    across = chips // 4
    steps = moves(regions)

    def swap(block, rank):
        if steps[rank] == (0, 0):
            return block
        pairs = [(i, target(i // 2, steps[rank], across) * 2 + i % 2) for i in range(regions)]
        return lax.ppermute(block, "region", pairs)

    def swap_core(block):
        return lax.ppermute(block, "region", [(i, i ^ 1) for i in range(regions)])

    live = jnp.arange(slots, dtype=jnp.int32) < active_slots[0]
    live_f = live.astype(jnp.float32)
    slot_site = jnp.where(live, measured_site, -1).astype(jnp.float32)
    table = spread(jnp.broadcast_to(slot_site[None, None], (regions, 1, slots)))
    facts = jnp.stack([measured_datum, inverse_variance * live_f])
    up = [(i, (i + 1) % regions) for i in range(regions)]
    down = [(target_, source) for source, target_ in up]
    facts = {
        -1: lax.ppermute(facts, "region", up), 0: facts, 1: lax.ppermute(facts, "region", down)
    }
    sites = table.astype(jnp.int32)
    cell = jnp.where(sites < 0, -1, sites % grid_sites)
    tier = jnp.where(sites < 0, -1, sites // grid_sites - tier_rank * tiers)
    observed = gather_observed(prior_samples, cell, tier, levels)
    flip = [(i, (i + 1) % levels) for i in range(levels)]
    observed = observed[0] + lax.ppermute(observed[1], "level", flip)
    observed = spread(observed)
    part = slots // levels
    observed = observed.reshape(regions * members, part)
    opposite = lax.ppermute(observed, "level", flip)
    sides = jnp.concatenate(
        [lax.ppermute(observed, "region", up), lax.ppermute(observed, "region", down)],
        axis=1,
    )
    window = jnp.concatenate(
        [observed, sides, opposite, lax.ppermute(sides, "level", flip)], axis=1
    )
    near = []
    for rank in (tier_rank, 1 - tier_rank):
        for shift in (0, -1, 1):
            start = rank * part
            site = lax.dynamic_slice(sites, ((me + shift) % regions, 0, start), (1, 1, part))[0, 0]
            value, weight = lax.dynamic_slice_in_dim(facts[shift], start, part, axis=1)
            here = (site >= 0).astype(jnp.float32)
            point = jnp.where(site < 0, 0, site % grid_sites).astype(jnp.float32)
            near.append(jnp.stack([value, weight, point + shift * grid_sites, here]))
    near = jnp.concatenate(near, axis=1)
    share = COARSE // levels
    coarse = (
        SPACING // 2 + SPACING * (tier_rank * share + jnp.arange(share, dtype=jnp.int32))
    ).astype(jnp.float32)
    gram_matrix, right_side = local_products(
        window, near, cutoff_distance[0].astype(jnp.float32), coarse
    )
    weights = ensemble_weights(gram_matrix, right_side)
    opposite = lax.ppermute(weights, "level", flip)
    before = lax.ppermute(jnp.where(tier_rank == 0, opposite, weights)[-1:], "region", up)
    beyond = lax.ppermute(jnp.where(tier_rank == 0, weights, opposite)[:1], "region", down)

    analysis = None
    early_count = -(-2 * (chips - 1) // 7)
    for half in range(HALVES):
        early = -(-(chips - 1) // 7) if half == 0 else 0
        pieces = []
        if early:
            pieces += cut(half, prior_samples, range(early), regions)
        pieces += cut(half, prior_samples, range(early, chips), regions)
        pieces = [swap(block, rank) for rank, block in enumerate(pieces)]
        other = hand(pieces)
        other = swap_core(other)
        edges = [] if half == 0 else [before, beyond]
        keep, give = transform(half, pieces, other, weights, opposite, edges)
        got = swap_core(give)
        blocks = pack(keep, got)
        blocks = [swap(block, rank) for rank, block in enumerate(blocks)]
        late = [] if half == 0 else list(range(chips - 1 - early_count, chips - 1))
        rest = [rank for rank in range(chips) if rank not in late]
        shape = prior_samples.shape
        analysis = join(half, blocks, shape, analysis, rest, regions)
        if late:
            analysis = join(half, blocks, shape, analysis, late, regions)
    return analysis


def solution(mesh):
    return jax.shard_map(
        analyse,
        mesh=mesh,
        in_specs=(
            P("region", "level", None),
            P("region"),
            P("region"),
            P("region"),
            P("region"),
            P("region"),
        ),
        out_specs=P("region", "level", None),
        check_vma=False,
    )
```

```python
import functools

import jax
import jax.numpy as jnp
from jax import lax
from jax.experimental import pallas as pl
from jax.experimental.pallas import tpu as pltpu
from jax.sharding import PartitionSpec as P


COARSE = 6
SPACING = 256
NS_ITERS = 5
HALVES = 2
LANES = 128

inflation = 1.1


def moves(regions):
    across = regions // 8
    steps = [(dz, dx) for dz in (3, 2, 1, 0) for dx in reversed(range(across))]
    turns = zip(steps[: 2 * across], steps[2 * across :])
    return [step for turn in turns for step in turn]


def target(chip, step, across):
    dz, dx = step
    return ((chip // across) ^ dz) * across + ((chip % across) ^ dx)


def standing(regions):
    across = regions // 8
    me = lax.axis_index("region")
    core = lax.rem(me, 2)
    row, column = lax.div(me, 2 * across), lax.rem(lax.div(me, 2), across)
    return core, [(row ^ dz) * across + (column ^ dx) for dz, dx in moves(regions)]


def gather_kernel(cell_ref, level_ref, fields_ref, out_ref):
    members, tiers, cells = fields_ref.shape
    slots = cell_ref.shape[-1]
    rows = lax.broadcasted_iota(jnp.int32, (cells, slots), 0)
    chosen = jnp.where(rows == cell_ref[0], 1.0, 0.0).astype(jnp.bfloat16)
    fields = fields_ref[...].reshape(members * tiers, cells)
    found = jnp.dot(fields, chosen, preferred_element_type=jnp.float32)
    found = found.reshape(members, tiers, slots)
    tier = lax.broadcasted_iota(jnp.int32, (members, tiers, slots), 1)
    found = jnp.where(tier == level_ref[...], found, 0.0)
    found = jnp.sum(found, axis=1).astype(jnp.bfloat16)
    levels, _, _, share = out_ref.shape
    rank = lax.axis_index("level")
    for h in range(levels):
        out_ref[lax.rem(h + rank, levels), 0] = found[:, h * share : (h + 1) * share]


def gather_observed(prior, cell, level, levels):
    members, tiers, total = prior.shape
    regions, _, slots = cell.shape
    cells = total // regions
    return pl.pallas_call(
        gather_kernel,
        grid=(regions,),
        in_specs=[
            pl.BlockSpec((1, 1, slots), lambda r: (r, 0, 0)),
            pl.BlockSpec((1, 1, slots), lambda r: (r, 0, 0)),
            pl.BlockSpec((members, tiers, cells), lambda r: (0, 0, r)),
        ],
        out_specs=pl.BlockSpec((levels, 1, members, slots // levels), lambda r: (0, r, 0, 0)),
        out_shape=jax.ShapeDtypeStruct(
            (levels, regions, members, slots // levels), jnp.bfloat16
        ),
        name="gather_observed",
    )(cell, level, prior)


def copy_all(reads, writes, arrived, left):
    share = len(reads) // len(writes)
    into = [pltpu.make_async_copy(a, b, arrived.at[i]) for i, (a, b) in enumerate(reads)]
    onward = [pltpu.make_async_copy(a, b, left.at[i]) for i, (a, b) in enumerate(writes)]
    for copy in into:
        copy.start()
    if share:
        for i, copy in enumerate(onward):
            for part in into[i * share : (i + 1) * share]:
                part.wait()
            copy.start()
    else:
        share = len(writes) // len(reads)
        for i, copy in enumerate(into):
            copy.wait()
            for part in onward[i * share : (i + 1) * share]:
                part.start()
    for copy in onward:
        copy.wait()


def moved(kernel, operands, out_shape, block, count, aliases=None):
    anywhere = pl.BlockSpec(memory_space=pl.ANY)
    several = isinstance(out_shape, list)
    return pl.pallas_call(
        kernel,
        in_specs=[anywhere] * len(operands),
        out_specs=[anywhere] * len(out_shape) if several else anywhere,
        out_shape=out_shape,
        scratch_shapes=[
            pltpu.VMEM((count,) + block, jnp.bfloat16),
            pltpu.SemaphoreType.DMA((2 * count,)),
            pltpu.SemaphoreType.DMA((2 * count,)),
        ],
        input_output_aliases=aliases or {},
    )(*operands)


def spans(half, cells):
    shift = SPACING // 2
    if half < HALVES - 1:
        return [(0, half * cells + shift, cells)]
    return [(0, half * cells + shift, cells - shift), (cells - shift, 0, shift)]


def cell_spans(chip, core, half, cells):
    region = chip * 2 + core
    for lane, cell, count in spans(half, cells):
        first = pl.multiple_of(region * (HALVES * cells) + cell, LANES)
        yield pl.ds(lane, count), pl.ds(first, count)


def cut(half, prior, ranks, regions):
    members, tiers, total = prior.shape
    cells = total // (regions * HALVES)
    shape = jax.ShapeDtypeStruct((2, members, tiers, cells), prior.dtype)

    def kernel(prior_ref, *refs):
        core, partners = standing(regions)
        reads, writes = [], []
        stage, arrived, left = refs[len(ranks) :]
        for i, rank in enumerate(ranks):
            for side in range(2):
                slot = stage.at[2 * i + side]
                for lanes, source in cell_spans(partners[rank], core ^ side, half, cells):
                    reads.append((prior_ref.at[:, :, source], slot.at[:, :, lanes]))
                writes.append((slot, refs[i].at[side]))
        copy_all(reads, writes, arrived, left)

    return moved(kernel, [prior], [shape] * len(ranks), shape.shape[1:], 2 * len(ranks))


def hand(pieces):
    chips = len(pieces)
    shape = jax.ShapeDtypeStruct((chips,) + pieces[0].shape[1:], pieces[0].dtype)

    def kernel(*refs):
        out_ref, stage, arrived, left = refs[chips:]
        copy_all(
            [(refs[p].at[1], stage.at[p]) for p in range(chips)],
            [(stage.at[p], out_ref.at[p]) for p in range(chips)],
            arrived,
            left,
        )

    return moved(kernel, pieces, shape, shape.shape[1:], chips)


def pack(keep, got):
    chips = keep.shape[0]
    shape = jax.ShapeDtypeStruct((2,) + keep.shape[1:], keep.dtype)

    def kernel(keep_ref, got_ref, *refs):
        stage, arrived, left = refs[chips:]
        reads, writes = [], []
        for p in range(chips):
            for side, source in enumerate((keep_ref, got_ref)):
                slot = stage.at[2 * p + side]
                reads.append((source.at[p], slot))
                writes.append((slot, refs[p].at[side]))
        copy_all(reads, writes, arrived, left)

    return moved(kernel, [keep, got], [shape] * chips, shape.shape[1:], 2 * chips)


def join(half, blocks, shape, base, ranks, regions):
    cells = blocks[0].shape[-1]
    operands = [blocks[rank] for rank in ranks] + ([] if base is None else [base])

    def kernel(*refs):
        core, partners = standing(regions)
        out_ref, stage, arrived, left = refs[len(operands) :]
        reads, writes = [], []
        for i, rank in enumerate(ranks):
            for side in range(2):
                slot = stage.at[2 * i + side]
                reads.append((refs[i].at[side], slot))
                for lanes, target in cell_spans(partners[rank], core ^ side, half, cells):
                    writes.append((slot.at[:, :, lanes], out_ref.at[:, :, target]))
        copy_all(reads, writes, arrived, left)

    aliases = None if base is None else {len(operands) - 1: 0}
    out = jax.ShapeDtypeStruct(shape, blocks[0].dtype)
    return moved(kernel, operands, out, blocks[0].shape[1:], 2 * len(ranks), aliases)


def transform_kernel(first, chips, *refs):
    pieces = refs[:chips]
    other_ref, own_ref, opposite_ref, *edges = refs[chips:-4]
    keep_ref, give_ref, work, matrices = refs[-4:]
    core, partners = standing(2 * chips)
    share = own_ref.shape[0]
    rank = lax.axis_index("level")
    for k in range(share):
        matrices[1 + rank * share + k] = own_ref[k]
        matrices[1 + (1 - rank) * share + k] = opposite_ref[k]
    for k, edge in enumerate(edges):
        matrices[((1 - rank) ^ k) * (2 * share + 1)] = edge[0]
    _, members, tiers, cells = other_ref.shape
    total = chips * 2 * members
    rows = members * tiers
    for p in range(chips):
        for side, piece in ((core, pieces[p][0]), (1 - core, other_ref[p])):
            start = pl.multiple_of((partners[p] * 2 + side) * rows, 8)
            piece = piece.astype(jnp.float32).reshape(rows, cells)
            for b in range(cells // LANES):
                work[b, pl.ds(start, rows), :] = piece[:, b * LANES : (b + 1) * LANES]
    offset = lax.broadcasted_iota(jnp.int32, (1, LANES), 1).astype(jnp.float32)
    half = SPACING // 2
    blocks = cells // LANES
    for b in range(blocks):
        block = (first * blocks + b + half // LANES) % (HALVES * blocks)
        skip = (block * LANES + half) % SPACING
        frac = (offset + skip) / SPACING
        frac = jnp.concatenate([frac] * tiers, axis=1)
        values = jnp.concatenate(
            [
                work[b, pl.ds(t, total, stride=tiers), :].astype(jnp.bfloat16)
                for t in range(tiers)
            ],
            axis=1,
        )
        base = (block * LANES + half) // SPACING
        under = jnp.dot(matrices[base], values, preferred_element_type=jnp.float32)
        over = jnp.dot(matrices[base + 1], values, preferred_element_type=jnp.float32)
        mixed = (1.0 - frac) * under + frac * over
        for t in range(tiers):
            work[b, pl.ds(t, total, stride=tiers), :] = mixed[:, t * LANES : (t + 1) * LANES]
    for p in range(chips):
        for side, out_ref in ((core, keep_ref), (1 - core, give_ref)):
            start = pl.multiple_of((partners[p] * 2 + side) * rows, 8)
            for b in range(blocks):
                block = work[b, pl.ds(start, rows), :].reshape(members, tiers, LANES)
                out_ref[p, :, :, b * LANES : (b + 1) * LANES] = block.astype(jnp.bfloat16)


def transform(first, pieces, other, own, opposite, edges):
    chips, members, tiers, cells = other.shape
    out = jax.ShapeDtypeStruct(other.shape, jnp.bfloat16)
    whole = pl.BlockSpec(memory_space=pltpu.VMEM)
    mine = pl.BlockSpec((1, members, tiers, cells), lambda i: (i, 0, 0, 0))
    return pl.pallas_call(
        functools.partial(transform_kernel, first, chips),
        grid=(1,),
        in_specs=[mine] * chips + [whole] * (3 + len(edges)),
        out_specs=[whole, whole],
        out_shape=[out, out],
        scratch_shapes=[
            pltpu.VMEM((cells // LANES, chips * 2 * members * tiers, LANES), jnp.float32),
            pltpu.VMEM((2 * own.shape[0] + 2,) + own.shape[1:], own.dtype),
        ],
    )(*pieces, other, own, opposite, *edges)


def local_products(window, records, radius_cells, coarse):
    values = window.astype(jnp.float32)
    centre = jnp.mean(values, axis=0)
    departure = values - centre[None, :]
    innovation = records[3] * (records[0] - centre)
    distance = (records[2][None, :] - coarse[:, None]) / radius_cells
    root_weight = jnp.sqrt(jnp.exp(-0.5 * distance * distance) * records[1][None, :])
    scaled = (departure[None, :, :] * root_weight[:, None, :]).astype(jnp.bfloat16)
    weighted = (root_weight * innovation[None, :]).astype(jnp.bfloat16)
    gram_matrix = jnp.einsum("cjo,cmo->cjm", scaled, scaled, preferred_element_type=jnp.float32)
    right_side = jnp.einsum("cjo,co->cj", scaled, weighted, preferred_element_type=jnp.float32)
    return (gram_matrix, right_side)


def ensemble_weights(gram_matrix, right_side):
    sample_runs = gram_matrix.shape[-1]
    identity = jnp.eye(sample_runs, dtype=jnp.float32)
    shifted = gram_matrix + (sample_runs - 1) / inflation * identity[None]
    frobenius = jnp.sqrt(jnp.sum(shifted * shifted, axis=(1, 2)))
    iterate = shifted / frobenius[:, None, None]
    inverse = 1.5 * identity[None] - 0.5 * iterate
    high = lax.Precision.HIGHEST
    iterate = jnp.matmul(iterate, inverse, precision=high)
    for turn in range(1, NS_ITERS):
        factor = 1.5 * identity[None] - 0.5 * jnp.matmul(inverse, iterate, precision=high)
        if turn < NS_ITERS - 1:
            iterate = jnp.matmul(iterate, factor, precision=high)
        inverse = jnp.matmul(factor, inverse, precision=high)
    spread = inverse * jnp.sqrt((sample_runs - 1.0) / frobenius)[:, None, None]
    inner_step = jnp.einsum("cjm,cm->cj", inverse, right_side, precision=high)
    centre = jnp.einsum("cjm,cm->cj", inverse, inner_step, precision=high) / frobenius[:, None]
    weights = spread + centre[:, :, None]
    weights = weights - jnp.mean(weights, axis=1, keepdims=True) + 1.0 / sample_runs
    return jnp.swapaxes(weights, 1, 2).astype(jnp.bfloat16)


def spread(block):
    return lax.all_to_all(block, "region", split_axis=0, concat_axis=0, tiled=True)


def analyse(
    prior_samples, measured_site, measured_datum, inverse_variance, active_slots, cutoff_distance
):
    members, tiers, _ = prior_samples.shape
    regions = lax.axis_size("region")
    levels = lax.axis_size("level")
    grid_sites = COARSE * SPACING
    slots = measured_site.shape[0]
    me = lax.axis_index("region")
    tier_rank = lax.axis_index("level")
    chips = regions // 2
    across = chips // 4
    steps = moves(regions)

    def swap(block, rank):
        if steps[rank] == (0, 0):
            return block
        pairs = [(i, target(i // 2, steps[rank], across) * 2 + i % 2) for i in range(regions)]
        return lax.ppermute(block, "region", pairs)

    def swap_core(block):
        return lax.ppermute(block, "region", [(i, i ^ 1) for i in range(regions)])

    live = jnp.arange(slots, dtype=jnp.int32) < active_slots[0]
    live_f = live.astype(jnp.float32)
    slot_site = jnp.where(live, measured_site, -1).astype(jnp.float32)
    table = spread(jnp.broadcast_to(slot_site[None, None], (regions, 1, slots)))
    facts = jnp.stack([measured_datum, inverse_variance * live_f])
    up = [(i, (i + 1) % regions) for i in range(regions)]
    down = [(target_, source) for source, target_ in up]
    facts = {
        -1: lax.ppermute(facts, "region", up), 0: facts, 1: lax.ppermute(facts, "region", down)
    }
    sites = table.astype(jnp.int32)
    cell = jnp.where(sites < 0, -1, sites % grid_sites)
    tier = jnp.where(sites < 0, -1, sites // grid_sites - tier_rank * tiers)
    observed = gather_observed(prior_samples, cell, tier, levels)
    flip = [(i, (i + 1) % levels) for i in range(levels)]
    observed = observed[0] + lax.ppermute(observed[1], "level", flip)
    observed = spread(observed)
    part = slots // levels
    observed = observed.reshape(regions * members, part)
    opposite = lax.ppermute(observed, "level", flip)
    sides = jnp.concatenate(
        [lax.ppermute(observed, "region", up), lax.ppermute(observed, "region", down)],
        axis=1,
    )
    window = jnp.concatenate(
        [observed, sides, opposite, lax.ppermute(sides, "level", flip)], axis=1
    )
    near = []
    for rank in (tier_rank, 1 - tier_rank):
        for shift in (0, -1, 1):
            start = rank * part
            site = lax.dynamic_slice(sites, ((me + shift) % regions, 0, start), (1, 1, part))[0, 0]
            value, weight = lax.dynamic_slice_in_dim(facts[shift], start, part, axis=1)
            here = (site >= 0).astype(jnp.float32)
            point = jnp.where(site < 0, 0, site % grid_sites).astype(jnp.float32)
            near.append(jnp.stack([value, weight, point + shift * grid_sites, here]))
    near = jnp.concatenate(near, axis=1)
    share = COARSE // levels
    coarse = (
        SPACING // 2 + SPACING * (tier_rank * share + jnp.arange(share, dtype=jnp.int32))
    ).astype(jnp.float32)
    gram_matrix, right_side = local_products(
        window, near, cutoff_distance[0].astype(jnp.float32), coarse
    )
    weights = ensemble_weights(gram_matrix, right_side)
    opposite = lax.ppermute(weights, "level", flip)
    pairs = [(r * levels, (r - 1) % regions * levels) for r in range(regions)]
    pairs += [(r * levels - 1, ((r % regions) + 1) * levels - 1) for r in range(1, regions + 1)]
    edge = lax.dynamic_slice_in_dim(weights, tier_rank * (share - 1), 1, axis=0)
    edge = lax.ppermute(edge, ("region", "level"), pairs)
    edges = [edge, lax.ppermute(edge, "level", flip)]

    analysis = None
    early_count = -(-(chips - 1) // 7)
    for half in range(HALVES):
        early = -(-(chips - 1) // 7) if half == 0 else 0
        pieces = []
        if early:
            pieces += cut(half, prior_samples, range(early), regions)
        pieces += cut(half, prior_samples, range(early, chips), regions)
        pieces = [swap(block, rank) for rank, block in enumerate(pieces)]
        other = hand(pieces)
        other = swap_core(other)
        keep, give = transform(half, pieces, other, weights, opposite, edges if half else [])
        got = swap_core(give)
        blocks = pack(keep, got)
        blocks = [swap(block, rank) for rank, block in enumerate(blocks)]
        late = [] if half == 0 else list(range(chips - 1 - early_count, chips - 1))
        rest = [rank for rank in range(chips) if rank not in late]
        shape = prior_samples.shape
        analysis = join(half, blocks, shape, analysis, rest, regions)
        if late:
            analysis = join(half, blocks, shape, analysis, late, regions)
    return analysis


def solution(mesh):
    return jax.shard_map(
        analyse,
        mesh=mesh,
        in_specs=(
            P("region", "level", None),
            P("region"),
            P("region"),
            P("region"),
            P("region"),
            P("region"),
        ),
        out_specs=P("region", "level", None),
        check_vma=False,
    )
```

```python
import functools

import jax
import jax.numpy as jnp
from jax import lax
from jax.experimental import pallas as pl
from jax.experimental.pallas import tpu as pltpu
from jax.sharding import PartitionSpec as P


COARSE = 6
SPACING = 256
NS_ITERS = 5
HALVES = 2
LANES = 128

inflation = 1.1


def moves(regions):
    across = regions // 8
    steps = [(dz, dx) for dz in (3, 2, 1, 0) for dx in reversed(range(across))]
    turns = zip(steps[: 2 * across], steps[2 * across :])
    return [step for turn in turns for step in turn]


def target(chip, step, across):
    dz, dx = step
    return ((chip // across) ^ dz) * across + ((chip % across) ^ dx)


def standing(regions):
    across = regions // 8
    me = lax.axis_index("region")
    core = lax.rem(me, 2)
    row, column = lax.div(me, 2 * across), lax.rem(lax.div(me, 2), across)
    return core, [(row ^ dz) * across + (column ^ dx) for dz, dx in moves(regions)]


def gather_kernel(cell_ref, level_ref, fields_ref, out_ref):
    members, tiers, cells = fields_ref.shape
    slots = cell_ref.shape[-1]
    rows = lax.broadcasted_iota(jnp.int32, (cells, slots), 0)
    chosen = jnp.where(rows == cell_ref[0], 1.0, 0.0).astype(jnp.bfloat16)
    fields = fields_ref[...].reshape(members * tiers, cells)
    found = jnp.dot(fields, chosen, preferred_element_type=jnp.float32)
    found = found.reshape(members, tiers, slots)
    tier = lax.broadcasted_iota(jnp.int32, (members, tiers, slots), 1)
    found = jnp.where(tier == level_ref[...], found, 0.0)
    found = jnp.sum(found, axis=1).astype(jnp.bfloat16)
    levels, _, _, share = out_ref.shape
    rank = lax.axis_index("level")
    for h in range(levels):
        out_ref[lax.rem(h + rank, levels), 0] = found[:, h * share : (h + 1) * share]


def gather_observed(prior, cell, level, levels):
    members, tiers, total = prior.shape
    regions, _, slots = cell.shape
    cells = total // regions
    return pl.pallas_call(
        gather_kernel,
        grid=(regions,),
        in_specs=[
            pl.BlockSpec((1, 1, slots), lambda r: (r, 0, 0)),
            pl.BlockSpec((1, 1, slots), lambda r: (r, 0, 0)),
            pl.BlockSpec((members, tiers, cells), lambda r: (0, 0, r)),
        ],
        out_specs=pl.BlockSpec((levels, 1, members, slots // levels), lambda r: (0, r, 0, 0)),
        out_shape=jax.ShapeDtypeStruct(
            (levels, regions, members, slots // levels), jnp.bfloat16
        ),
        name="gather_observed",
    )(cell, level, prior)


def copy_all(reads, writes, arrived, left):
    share = len(reads) // len(writes)
    into = [pltpu.make_async_copy(a, b, arrived.at[i]) for i, (a, b) in enumerate(reads)]
    onward = [pltpu.make_async_copy(a, b, left.at[i]) for i, (a, b) in enumerate(writes)]
    for copy in into:
        copy.start()
    if share:
        for i, copy in enumerate(onward):
            for part in into[i * share : (i + 1) * share]:
                part.wait()
            copy.start()
    else:
        share = len(writes) // len(reads)
        for i, copy in enumerate(into):
            copy.wait()
            for part in onward[i * share : (i + 1) * share]:
                part.start()
    for copy in onward:
        copy.wait()


def moved(kernel, operands, out_shape, block, count, aliases=None):
    anywhere = pl.BlockSpec(memory_space=pl.ANY)
    several = isinstance(out_shape, list)
    return pl.pallas_call(
        kernel,
        in_specs=[anywhere] * len(operands),
        out_specs=[anywhere] * len(out_shape) if several else anywhere,
        out_shape=out_shape,
        scratch_shapes=[
            pltpu.VMEM((count,) + block, jnp.bfloat16),
            pltpu.SemaphoreType.DMA((2 * count,)),
            pltpu.SemaphoreType.DMA((2 * count,)),
        ],
        input_output_aliases=aliases or {},
    )(*operands)


def spans(half, cells):
    shift = SPACING // 2
    if half < HALVES - 1:
        return [(0, half * cells + shift, cells)]
    return [(0, half * cells + shift, cells - shift), (cells - shift, 0, shift)]


def cell_spans(chip, core, half, cells):
    region = chip * 2 + core
    for lane, cell, count in spans(half, cells):
        first = pl.multiple_of(region * (HALVES * cells) + cell, LANES)
        yield pl.ds(lane, count), pl.ds(first, count)


def cut(half, prior, ranks, regions):
    members, tiers, total = prior.shape
    cells = total // (regions * HALVES)
    shape = jax.ShapeDtypeStruct((2, members, tiers, cells), prior.dtype)

    def kernel(prior_ref, *refs):
        core, partners = standing(regions)
        reads, writes = [], []
        stage, arrived, left = refs[len(ranks) :]
        for i, rank in enumerate(ranks):
            for side in range(2):
                slot = stage.at[2 * i + side]
                for lanes, source in cell_spans(partners[rank], core ^ side, half, cells):
                    reads.append((prior_ref.at[:, :, source], slot.at[:, :, lanes]))
                writes.append((slot, refs[i].at[side]))
        copy_all(reads, writes, arrived, left)

    return moved(kernel, [prior], [shape] * len(ranks), shape.shape[1:], 2 * len(ranks))


def hand(pieces):
    chips = len(pieces)
    shape = jax.ShapeDtypeStruct((chips,) + pieces[0].shape[1:], pieces[0].dtype)

    def kernel(*refs):
        out_ref, stage, arrived, left = refs[chips:]
        copy_all(
            [(refs[p].at[1], stage.at[p]) for p in range(chips)],
            [(stage.at[p], out_ref.at[p]) for p in range(chips)],
            arrived,
            left,
        )

    return moved(kernel, pieces, shape, shape.shape[1:], chips)


def pack(keep, got):
    chips = keep.shape[0]
    shape = jax.ShapeDtypeStruct((2,) + keep.shape[1:], keep.dtype)

    def kernel(keep_ref, got_ref, *refs):
        stage, arrived, left = refs[chips:]
        reads, writes = [], []
        for p in range(chips):
            for side, source in enumerate((keep_ref, got_ref)):
                slot = stage.at[2 * p + side]
                reads.append((source.at[p], slot))
                writes.append((slot, refs[p].at[side]))
        copy_all(reads, writes, arrived, left)

    return moved(kernel, [keep, got], [shape] * chips, shape.shape[1:], 2 * chips)


def join(half, blocks, shape, base, ranks, regions):
    cells = blocks[0].shape[-1]
    operands = [blocks[rank] for rank in ranks] + ([] if base is None else [base])

    def kernel(*refs):
        core, partners = standing(regions)
        out_ref, stage, arrived, left = refs[len(operands) :]
        reads, writes = [], []
        for i, rank in enumerate(ranks):
            for side in range(2):
                slot = stage.at[2 * i + side]
                reads.append((refs[i].at[side], slot))
                for lanes, target in cell_spans(partners[rank], core ^ side, half, cells):
                    writes.append((slot.at[:, :, lanes], out_ref.at[:, :, target]))
        copy_all(reads, writes, arrived, left)

    aliases = None if base is None else {len(operands) - 1: 0}
    out = jax.ShapeDtypeStruct(shape, blocks[0].dtype)
    return moved(kernel, operands, out, blocks[0].shape[1:], 2 * len(ranks), aliases)


def transform_kernel(first, chips, *refs):
    pieces = refs[:chips]
    other_ref, own_ref, opposite_ref, *edges = refs[chips:-4]
    keep_ref, give_ref, work, matrices = refs[-4:]
    core, partners = standing(2 * chips)
    share = own_ref.shape[0]
    rank = lax.axis_index("level")
    for k in range(share):
        matrices[1 + rank * share + k] = own_ref[k]
        matrices[1 + (1 - rank) * share + k] = opposite_ref[k]
    for k, edge in enumerate(edges):
        matrices[((1 - rank) ^ k) * (2 * share + 1)] = edge[0]
    _, members, tiers, cells = other_ref.shape
    total = chips * 2 * members
    rows = members * tiers
    for p in range(chips):
        for side, piece in ((core, pieces[p][0]), (1 - core, other_ref[p])):
            start = pl.multiple_of((partners[p] * 2 + side) * rows, 8)
            piece = piece.astype(jnp.float32).reshape(rows, cells)
            for b in range(cells // LANES):
                work[b, pl.ds(start, rows), :] = piece[:, b * LANES : (b + 1) * LANES]
    offset = lax.broadcasted_iota(jnp.int32, (1, LANES), 1).astype(jnp.float32)
    half = SPACING // 2
    blocks = cells // LANES
    for b in range(blocks):
        block = (first * blocks + b + half // LANES) % (HALVES * blocks)
        skip = (block * LANES + half) % SPACING
        frac = (offset + skip) / SPACING
        frac = jnp.concatenate([frac] * tiers, axis=1)
        values = jnp.concatenate(
            [
                work[b, pl.ds(t, total, stride=tiers), :].astype(jnp.bfloat16)
                for t in range(tiers)
            ],
            axis=1,
        )
        base = (block * LANES + half) // SPACING
        under = jnp.dot(matrices[base], values, preferred_element_type=jnp.float32)
        over = jnp.dot(matrices[base + 1], values, preferred_element_type=jnp.float32)
        mixed = (1.0 - frac) * under + frac * over
        for t in range(tiers):
            work[b, pl.ds(t, total, stride=tiers), :] = mixed[:, t * LANES : (t + 1) * LANES]
    for p in range(chips):
        for side, out_ref in ((core, keep_ref), (1 - core, give_ref)):
            start = pl.multiple_of((partners[p] * 2 + side) * rows, 8)
            for b in range(blocks):
                block = work[b, pl.ds(start, rows), :].reshape(members, tiers, LANES)
                out_ref[p, :, :, b * LANES : (b + 1) * LANES] = block.astype(jnp.bfloat16)


def transform(first, pieces, other, own, opposite, edges):
    chips, members, tiers, cells = other.shape
    out = jax.ShapeDtypeStruct(other.shape, jnp.bfloat16)
    whole = pl.BlockSpec(memory_space=pltpu.VMEM)
    mine = pl.BlockSpec((1, members, tiers, cells), lambda i: (i, 0, 0, 0))
    return pl.pallas_call(
        functools.partial(transform_kernel, first, chips),
        grid=(1,),
        in_specs=[mine] * chips + [whole] * (3 + len(edges)),
        out_specs=[whole, whole],
        out_shape=[out, out],
        scratch_shapes=[
            pltpu.VMEM((cells // LANES, chips * 2 * members * tiers, LANES), jnp.float32),
            pltpu.VMEM((2 * own.shape[0] + 2,) + own.shape[1:], own.dtype),
        ],
    )(*pieces, other, own, opposite, *edges)


def local_products(window, records, radius_cells, coarse):
    values = window.astype(jnp.float32)
    centre = jnp.mean(values, axis=0)
    departure = values - centre[None, :]
    innovation = records[3] * (records[0] - centre)
    distance = (records[2][None, :] - coarse[:, None]) / radius_cells
    root_weight = jnp.sqrt(jnp.exp(-0.5 * distance * distance) * records[1][None, :])
    scaled = (departure[None, :, :] * root_weight[:, None, :]).astype(jnp.bfloat16)
    weighted = (root_weight * innovation[None, :]).astype(jnp.bfloat16)
    gram_matrix = jnp.einsum("cjo,cmo->cjm", scaled, scaled, preferred_element_type=jnp.float32)
    right_side = jnp.einsum("cjo,co->cj", scaled, weighted, preferred_element_type=jnp.float32)
    return (gram_matrix, right_side)


def ensemble_weights(gram_matrix, right_side):
    sample_runs = gram_matrix.shape[-1]
    identity = jnp.eye(sample_runs, dtype=jnp.float32)
    shifted = gram_matrix + (sample_runs - 1) / inflation * identity[None]
    frobenius = jnp.sqrt(jnp.sum(shifted * shifted, axis=(1, 2)))
    iterate = shifted / frobenius[:, None, None]
    inverse = 1.5 * identity[None] - 0.5 * iterate
    high = lax.Precision.HIGHEST
    iterate = jnp.matmul(iterate, inverse, precision=high)
    for turn in range(1, NS_ITERS):
        factor = 1.5 * identity[None] - 0.5 * jnp.matmul(inverse, iterate, precision=high)
        if turn < NS_ITERS - 1:
            iterate = jnp.matmul(iterate, factor, precision=high)
        inverse = jnp.matmul(factor, inverse, precision=high)
    spread = inverse * jnp.sqrt((sample_runs - 1.0) / frobenius)[:, None, None]
    inner_step = jnp.einsum("cjm,cm->cj", inverse, right_side, precision=high)
    centre = jnp.einsum("cjm,cm->cj", inverse, inner_step, precision=high) / frobenius[:, None]
    weights = spread + centre[:, :, None]
    weights = weights - jnp.mean(weights, axis=1, keepdims=True) + 1.0 / sample_runs
    return jnp.swapaxes(weights, 1, 2).astype(jnp.bfloat16)


def spread(block):
    return lax.all_to_all(block, "region", split_axis=0, concat_axis=0, tiled=True)


def analyse(
    prior_samples, measured_site, measured_datum, inverse_variance, active_slots, cutoff_distance
):
    members, tiers, _ = prior_samples.shape
    regions = lax.axis_size("region")
    levels = lax.axis_size("level")
    grid_sites = COARSE * SPACING
    slots = measured_site.shape[0]
    me = lax.axis_index("region")
    tier_rank = lax.axis_index("level")
    chips = regions // 2
    across = chips // 4
    steps = moves(regions)

    def swap(block, rank):
        if steps[rank] == (0, 0):
            return block
        pairs = [(i, target(i // 2, steps[rank], across) * 2 + i % 2) for i in range(regions)]
        return lax.ppermute(block, "region", pairs)

    def swap_core(block):
        return lax.ppermute(block, "region", [(i, i ^ 1) for i in range(regions)])

    live = jnp.arange(slots, dtype=jnp.int32) < active_slots[0]
    live_f = live.astype(jnp.float32)
    slot_site = jnp.where(live, measured_site, -1).astype(jnp.float32)
    table = spread(jnp.broadcast_to(slot_site[None, None], (regions, 1, slots)))
    facts = jnp.stack([measured_datum, inverse_variance * live_f])
    up = [(i, (i + 1) % regions) for i in range(regions)]
    down = [(target_, source) for source, target_ in up]
    facts = {
        -1: lax.ppermute(facts, "region", up), 0: facts, 1: lax.ppermute(facts, "region", down)
    }
    sites = table.astype(jnp.int32)
    cell = jnp.where(sites < 0, -1, sites % grid_sites)
    tier = jnp.where(sites < 0, -1, sites // grid_sites - tier_rank * tiers)
    observed = gather_observed(prior_samples, cell, tier, levels)
    flip = [(i, (i + 1) % levels) for i in range(levels)]
    observed = observed[0] + lax.ppermute(observed[1], "level", flip)
    observed = spread(observed)
    part = slots // levels
    observed = observed.reshape(regions * members, part)
    opposite = lax.ppermute(observed, "level", flip)
    sides = jnp.concatenate(
        [lax.ppermute(observed, "region", up), lax.ppermute(observed, "region", down)],
        axis=1,
    )
    window = jnp.concatenate(
        [observed, sides, opposite, lax.ppermute(sides, "level", flip)], axis=1
    )
    near = []
    for rank in (tier_rank, 1 - tier_rank):
        for shift in (0, -1, 1):
            start = rank * part
            site = lax.dynamic_slice(sites, ((me + shift) % regions, 0, start), (1, 1, part))[0, 0]
            value, weight = lax.dynamic_slice_in_dim(facts[shift], start, part, axis=1)
            here = (site >= 0).astype(jnp.float32)
            point = jnp.where(site < 0, 0, site % grid_sites).astype(jnp.float32)
            near.append(jnp.stack([value, weight, point + shift * grid_sites, here]))
    near = jnp.concatenate(near, axis=1)
    share = COARSE // levels
    coarse = (
        SPACING // 2 + SPACING * (tier_rank * share + jnp.arange(share, dtype=jnp.int32))
    ).astype(jnp.float32)
    gram_matrix, right_side = local_products(
        window, near, cutoff_distance[0].astype(jnp.float32), coarse
    )
    weights = ensemble_weights(gram_matrix, right_side)
    opposite = lax.ppermute(weights, "level", flip)
    pairs = [(r * levels, (r - 1) % regions * levels) for r in range(regions)]
    pairs += [(r * levels - 1, ((r % regions) + 1) * levels - 1) for r in range(1, regions + 1)]
    edge = lax.dynamic_slice_in_dim(weights, tier_rank * (share - 1), 1, axis=0)
    edge = lax.ppermute(edge, ("region", "level"), pairs)
    edges = [edge, lax.ppermute(edge, "level", flip)]

    analysis = None
    early_count = -(-(chips - 1) // 7)
    for half in range(HALVES):
        early = -(-(chips - 1) // 7) if half == 0 else 0
        pieces = []
        if early:
            pieces += cut(half, prior_samples, range(early), regions)
        pieces += cut(half, prior_samples, range(early, chips), regions)
        pieces = [swap(block, rank) for rank, block in enumerate(pieces)]
        other = hand(pieces)
        other = swap_core(other)
        keep, give = transform(half, pieces, other, weights, opposite, edges if half else [])
        got = swap_core(give)
        blocks = pack(keep, got)
        blocks = [swap(block, rank) for rank, block in enumerate(blocks)]
        late = [] if half == 0 else list(range(chips - 1 - early_count, chips - 1))
        rest = [rank for rank in range(chips) if rank not in late]
        shape = prior_samples.shape
        analysis = join(half, blocks, shape, analysis, rest, regions)
        if late:
            core, partners = standing(regions)
            for rank in late:
                for side in range(2):
                    first = (partners[rank] * 2 + (core ^ side)) * grid_sites
                    for lane, cell, count in spans(half, blocks[rank].shape[-1]):
                        analysis = lax.dynamic_update_slice_in_dim(
                            analysis,
                            blocks[rank][side, :, :, lane : lane + count],
                            first + cell,
                            axis=2,
                        )
    return analysis


def solution(mesh):
    return jax.shard_map(
        analyse,
        mesh=mesh,
        in_specs=(
            P("region", "level", None),
            P("region"),
            P("region"),
            P("region"),
            P("region"),
            P("region"),
        ),
        out_specs=P("region", "level", None),
        check_vma=False,
    )
```
